32 devices in a mesh: tm: 8 (over y, x, core), group: 4 (over z).
Axes of the slice: x: 2, y: 2, z: 4, core: 2. Of those that a mesh axis runs over, the one named last changes fastest.
Arguments:
- frames: bfloat16 [4, 65536, 512], P('group', 'tm')
- pair_count: int32 [4], P('group'), may hold values from 32768 to 63488, as said below
Outputs:
- group_instant: float32 [4, 512, 512], P('group', 'tm')
- group_lagged: float32 [4, 512, 512], P('group', 'tm')
- pooled_instant: float32 [512, 512], P('tm')
- pooled_lagged: float32 [512, 512], P('tm')
The draws below stay inside these ranges and needn't reach their ends.
Inputs may be any that keep to these rules, and one draw needn't show every extreme that they name: `pair_count`: every session has between 32768 and 63488 pairs, and some session has exactly 63488.
All inputs are finite; a program needn't handle non-finite values.
Results may differ from the reference program's by a relative error of at most 0.0003.
Values may be sent and summed in bfloat16 or wider, within the bound.
A program may use at most 64 MiB of HBM per device.

```python
import math
import jax
import jax.numpy as jnp
from jax import lax

F = 512
LAG = 2048
FRAMES_SEQ = 65536
GROUPS = 4


def draw_frames(key, part):
    modes = 64
    keys = jax.random.split(key, 5)
    freq = jnp.exp(jax.random.uniform(keys[0], (modes,), jnp.float32, math.log(2.0 * math.pi / (4.0 * LAG)), math.log(2.0 * math.pi / 16.0)))
    phase = jax.random.uniform(keys[1], (GROUPS, modes), jnp.float32, 0.0, 2.0 * math.pi)
    mixing = jax.random.normal(keys[2], (modes, F), jnp.float32) / math.sqrt(128.0)
    offset = 0.5 * jax.random.normal(keys[3], (GROUPS, F), jnp.float32)
    times = jnp.arange(FRAMES_SEQ, dtype=jnp.float32)
    envelope = 1.0 + 2.0 * times / FRAMES_SEQ

    def one_session(index):
        waves = jnp.sin(times[:, None] * freq[None] + phase[index][None])
        signal = jnp.dot(waves, mixing) * envelope[:, None]
        noise = jax.random.normal(jax.random.fold_in(keys[4], index), (FRAMES_SEQ, F), jnp.float32)
        return (signal + noise + offset[index][None]).astype(jnp.bfloat16)
    return lax.map(one_session, jnp.arange(GROUPS, dtype=jnp.int32))


def draw_pair_count(key, part):
    keys = jax.random.split(jax.random.fold_in(key, 17), 2)
    lowest = FRAMES_SEQ // 2
    highest = FRAMES_SEQ - LAG
    values = jax.random.randint(keys[0], (GROUPS,), lowest, highest + 1, jnp.int32)
    which = jax.random.randint(keys[1], (), 0, GROUPS, jnp.int32)
    return jnp.where(jnp.arange(GROUPS, dtype=jnp.int32) == which, highest, values).astype(jnp.int32)


def setup_inputs(seed: int = 0) -> dict:
    arg_keys = jax.random.split(jax.random.key(seed), 3)
    frames = draw_frames(jax.random.fold_in(arg_keys[2], 71), 0)
    pair_count = draw_pair_count(jax.random.fold_in(arg_keys[2], 71), 0)
    return dict(frames=frames, pair_count=pair_count)


def per_group(item):
    block, count = item
    span = FRAMES_SEQ - LAG
    wide = block[:span].astype(jnp.float32)
    later = block[LAG:].astype(jnp.float32)
    weight = (jnp.arange(span, dtype=jnp.int32) < count).astype(jnp.float32)[:, None]
    number = count.astype(jnp.float32)
    sum_x = jnp.sum(wide * weight, axis=0)
    sum_y = jnp.sum(later * weight, axis=0)
    cent_x = (wide - sum_x / number) * weight
    cent_y = (later - sum_y / number) * weight
    inst = jnp.dot(cent_x.T, cent_x, precision=lax.Precision.HIGHEST, preferred_element_type=jnp.float32)
    lagm = jnp.dot(cent_x.T, cent_y, precision=lax.Precision.HIGHEST, preferred_element_type=jnp.float32)
    return inst, lagm, sum_x, sum_y


def reference(frames, pair_count):
    inst, lagm, sum_x, sum_y = lax.map(per_group, (frames, pair_count))
    number = pair_count.astype(jnp.float32)
    group_instant = inst / number[:, None, None]
    group_lagged = lagm / number[:, None, None]
    total = jnp.sum(number)
    mean_x = sum_x / number[:, None]
    mean_y = sum_y / number[:, None]
    glob_x = jnp.sum(sum_x, axis=0) / total
    glob_y = jnp.sum(sum_y, axis=0) / total
    dev_x = mean_x - glob_x[None]
    dev_y = mean_y - glob_y[None]
    spread_i = jnp.einsum("g,gi,gj->ij", number, dev_x, dev_x, precision=lax.Precision.HIGHEST)
    spread_l = jnp.einsum("g,gi,gj->ij", number, dev_x, dev_y, precision=lax.Precision.HIGHEST)
    pooled_instant = (jnp.sum(inst, axis=0) + spread_i) / total
    pooled_lagged = (jnp.sum(lagm, axis=0) + spread_l) / total
    return group_instant, group_lagged, pooled_instant, pooled_lagged
```

```python
import functools

import jax
import jax.numpy as jnp
from jax import lax
from jax.experimental import pallas as pl
from jax.experimental.pallas import tpu as pltpu
from jax.sharding import PartitionSpec as P

LAG = 2048
MESH = pl.DeviceIdType.MESH
PAD = 16
CUTS = 4
PIECES = 2
LANES = 128
LEVELS = 32700.0
STEPS = 8.0
LEAST = 1e-30


def encode(ref, block):
    S, W = block.shape
    top = jnp.maximum(jnp.max(jnp.abs(block), axis=0, keepdims=True), LEAST)
    power = jnp.ceil(STEPS * jnp.log2(top * (1.0 / LEVELS)))
    codes = jnp.round(block * (1.0 / jnp.exp2(power * (1.0 / STEPS))))
    ref[0:S, :] = codes.astype(jnp.int32).astype(jnp.int16)
    ref[S:, :] = jnp.broadcast_to(power, (PAD, W)).astype(jnp.int32).astype(jnp.int16)


def decode(ref):
    S = ref.shape[0] - PAD
    codes = ref[0:S, :].astype(jnp.int32).astype(jnp.float32)
    power = ref[S:, :].astype(jnp.int32).astype(jnp.float32)[0:1]
    return codes * jnp.exp2(power * (1.0 / STEPS))


def wide(column, width):
    return jnp.concatenate([column] * (width // LANES), axis=1)


def kernel(
    T, G, count_ref, frames_ref, gi_ref, gl_ref, pi_ref, po_ref,
    x, xt, head, tail, acc, ai, al, r1i, r1l, qi, ri, ql, rl, zi, zl,
    s_own, s_mate, s_chip, s_grp, cols, fix,
    ld, hs, hr, s1, e1, s2i, e2i, s2l, e2l, szi, ezi, szl, ezl, ssm, esm, ssc, esc, ssz, esz,
):
    F = frames_ref.shape[2]
    R = frames_ref.shape[1]
    H = LAG // CUTS
    NB = R // H
    W = F // PIECES
    S = F // T
    Q = T // 2
    FR = F // LANES
    f32 = jnp.float32
    me = lax.axis_index("tm")
    z = lax.axis_index("group")
    c = lax.rem(me, 2)
    q = lax.div(me, 2)
    partner = me + 1 - 2 * c
    count = count_ref[0]

    def remote(src, dst, a, b, dev):
        return pltpu.make_async_remote_copy(
            src_ref=src, dst_ref=dst, send_sem=a, recv_sem=b,
            device_id=dev, device_id_type=MESH,
        )

    def load(i):
        return pltpu.make_async_copy(frames_ref.at[0, pl.ds(i * H, H)], x.at[i], ld.at[i])

    for i in range(NB):
        load(i).start()

    barrier = pltpu.get_barrier_semaphore()
    for k in range(1, T):
        pl.semaphore_signal(
            barrier, inc=1, device_id={"tm": lax.rem(me + k, T)}, device_id_type=MESH
        )
    for k in range(1, G):
        pl.semaphore_signal(
            barrier, inc=1, device_id={"group": lax.rem(z + k, G)}, device_id_type=MESH
        )
    with jax.named_scope("t_barrier"):
        pl.semaphore_wait(barrier, T - 1 + G - 1)

    def kept(b):
        if T != 8:
            return CUTS // 2
        turn = lax.rem(b, 2) * (1 - lax.rem(lax.div(b, 2), 2))
        return CUTS // 2 + turn * (2 * lax.div(b, 4) - 1)

    before = lax.rem(me + T - 1, T)

    def send_head(j):
        return remote(
            frames_ref.at[0, pl.ds(j * H, H)], head.at[j], hs.at[0, j], hr.at[0, j], {"tm": me - 1}
        )

    def send_tail(j):
        return remote(
            frames_ref.at[0, pl.ds(R - LAG + j * H, H)], tail.at[j], hs.at[1, j], hr.at[1, j],
            {"tm": me + 1},
        )

    def sent(act):
        for j in range(CUTS):
            @pl.when((me > 0) & (j < kept(before)))
            def _():
                act(send_head(j))

            @pl.when((me < T - 1) & (j >= kept(me)))
            def _():
                act(send_tail(j))

    sent(lambda copy: copy.start())

    def put_transposed(block, base, slot):
        rows = lax.broadcasted_iota(jnp.int32, (H, LANES), 0) + base
        keep = jnp.where(rows < count, 1.0, 0.0).astype(jnp.bfloat16)
        xt[slot, 0:F, :] = (block * wide(keep, F)).T

    def put_masks(base, slot):
        frame = lax.broadcasted_iota(jnp.int32, (PAD, H), 1) + base
        kind = lax.broadcasted_iota(jnp.int32, (PAD, H), 0)
        first = jnp.where(kind == 0, 0, LAG)
        valid = (frame >= first) & (frame < first + count) & (kind < 2)
        xt[slot, F:, :] = jnp.where(valid, 1.0, 0.0).astype(jnp.bfloat16)

    def product(slot, block):
        return jnp.dot(xt[slot, 0:F, :], block, preferred_element_type=f32)

    acc[...] = jnp.zeros_like(acc)

    def inst_step(i, carry):
        for j in (2 * i, 2 * i + 1):
            load(j).wait()
            put_transposed(x[j], me * R + j * H, j)
            put_masks(me * R + j * H, j)
        acc[...] += (
            jnp.dot(xt[2 * i], x[2 * i], preferred_element_type=f32)
            + jnp.dot(xt[2 * i + 1], x[2 * i + 1], preferred_element_type=f32)
        )
        return carry

    with jax.named_scope("t_inst"):
        lax.fori_loop(0, NB // 2, inst_step, 0)
    for d in range(T):
        ai[d % 2, d // 2] = acc[d * S:(d + 1) * S, :]
    for k in range(2):
        for j in range(FR):
            s_own[k * FR + j:k * FR + j + 1, :] = acc[F + k:F + k + 1, j * LANES:(j + 1) * LANES]
    p1i = remote(ai.at[1 - c], r1i, s1.at[0], e1.at[0], {"tm": partner})
    p1i.start()
    mate = remote(s_own, s_mate, ssm.at[0], esm.at[0], {"tm": partner})
    mate.start()

    acc[...] = jnp.zeros_like(acc)

    def lag_step(i, carry):
        j = 2 * i
        acc[0:F, :] += product(j, x[j + CUTS]) + product(j + 1, x[j + 1 + CUTS])
        return carry

    with jax.named_scope("t_lag"):
        lax.fori_loop(0, (NB - CUTS) // 2, lag_step, 0)

    def clip(v, top):
        return jnp.minimum(jnp.maximum(v, 0), top)

    def vector(n):
        return jnp.broadcast_to(n, (1, LANES)).astype(f32)

    def weights(chip):
        a = chip * 2 * R
        nx = clip(count - a, 2 * R)
        ny = clip(count + LAG - a, 2 * R) - clip(LAG - a, 2 * R)
        low = jnp.where(chip > 0, kept(2 * chip - 1) * H - LAG, 0)
        high = jnp.where(chip < Q - 1, kept(2 * chip + 1) * H - LAG, 0)
        pairs = clip(count - a - low, 2 * R + high - low)
        vx, vy = vector(jnp.maximum(nx, 1)), vector(jnp.maximum(ny, 1))
        return 1.0 / vx, vector(pairs) / (vx * vy)

    lanes = lax.broadcasted_iota(jnp.int32, (S, LANES), 1)
    rows = lax.broadcasted_iota(jnp.int32, (S, LANES), 0)

    def upright(row, offset):
        picked = jnp.where(lanes == rows + offset, jnp.broadcast_to(row, (S, LANES)), 0.0)
        return jnp.broadcast_to(jnp.sum(picked, axis=1, keepdims=True), (S, LANES))

    def along(ref, kind):
        return jnp.concatenate([ref[kind * FR + j:kind * FR + j + 1, :] for j in range(FR)], axis=1)

    with jax.named_scope("t_p1i"):
        mate.wait_recv()
        s_chip[q] = s_own[...] + s_mate[...]
        chips = [
            remote(s_chip.at[q], s_chip.at[q], ssc.at[k - 1], esc.at[k - 1],
                   {"tm": 2 * lax.rem(q + k, Q) + c})
            for k in range(1, Q)
        ]
        for copy in chips:
            copy.start()
        wx, wl = weights(q)
        mine = s_chip.at[q]
        for k in range(Q):
            at = 2 * k * S
            col = upright(mine[at // LANES:at // LANES + 1, :], at % LANES + c * S)
            cols[0, k] = col * wx
            cols[1, k] = col * wl
        p1i.wait_recv()
        sx = along(mine, 0)
        for k in range(Q):
            ai[c, k] = ai[c, k] + r1i[k] - wide(cols[0, k], F) * sx

    square = Q == 4
    with jax.named_scope("t_inst_send"):
        if square:
            side, level = lax.rem(q, 2), lax.div(q, 2)
            across = q + 1 - 2 * side
            for k in range(2):
                encode(qi.at[k], ai[c, 2 - 2 * level + k])
            over = remote(
                qi.at[pl.ds(0, 2)], ri.at[pl.ds(0, 2)], s2i.at[0], e2i.at[0],
                {"tm": 2 * lax.rem(q + 2, Q) + c},
            )
            over.start()
            p2i = [remote(qi.at[2], ri.at[2], s2i.at[1], e2i.at[1], {"tm": 2 * across + c})]
        else:
            over = None
            p2i = []
            for k in range(1, Q):
                q2 = lax.rem(q + k, Q)
                encode(qi.at[k - 1], ai[c, q2])
                p2i.append(remote(
                    qi.at[k - 1], ri.at[k - 1], s2i.at[k - 1], e2i.at[k - 1], {"tm": 2 * q2 + c}
                ))
                p2i[-1].start()

    def heads():
        def head_step(j, carry):
            send_head(j).wait_recv()
            acc[0:F, :] += product(NB - CUTS + j, head[j])
            return carry

        lax.fori_loop(0, kept(me), head_step, 0)

    def tails():
        def tail_step(j, carry):
            send_tail(j).wait_recv()
            put_transposed(tail[j], me * R - LAG + j * H, j)
            acc[0:F, :] += product(j, x[j])
            return carry

        lax.fori_loop(kept(before), CUTS, tail_step, 0)

    with jax.named_scope("t_halo_near"):
        pl.when(c == 0)(heads)
        pl.when(c == 1)(tails)

    with jax.named_scope("t_inst_x"):
        if square:
            over.wait_recv()
            for k in range(2):
                ai[c, 2 * level + k] += decode(ri.at[k])
            encode(qi.at[2], ai[c, across])
            p2i[0].start()

    with jax.named_scope("t_halo_far"):
        pl.when((me < T - 1) & (c == 1))(heads)
        pl.when((me > 0) & (c == 0))(tails)

    with jax.named_scope("t_lag_out"):
        p1l = []
        for h in range(PIECES):
            for d in range(T):
                al[h, d % 2, d // 2] = acc[d * S:(d + 1) * S, h * W:(h + 1) * W]
            p1l.append(
                remote(al.at[h, 1 - c], r1l.at[h], s1.at[1 + h], e1.at[1 + h], {"tm": partner})
            )
            p1l[h].start()

    with jax.named_scope("t_sums"):
        for copy in chips:
            copy.wait_recv()

        at = lax.div(me * S, LANES)
        off = lax.rem(me * S, LANES)

        def outer(ref, kind, scale):
            return wide(upright(ref[pl.ds(at, 1), :], off) * scale, F) * along(ref, kind)

        total = s_chip[0]
        for k in range(1, Q):
            total = total + s_chip[k]
        s_grp[z, 0:2 * FR, :] = total
        s_grp[z, 2 * FR:, :] = jnp.broadcast_to(vector(count), (8, LANES))
        groups = [
            remote(s_grp.at[z], s_grp.at[z], ssz.at[k - 1], esz.at[k - 1],
                   {"group": lax.rem(z + k, G)})
            for k in range(1, G)
        ]
        for copy in groups:
            copy.start()
        number = vector(count)
        for kind in range(2):
            term = -outer(s_grp.at[z], kind, 1.0 / number)
            for k in range(Q):
                term = term + outer(s_chip.at[k], kind, weights(k)[kind])
            fix[kind] = term

    with jax.named_scope("t_p1l"):
        p2l = [[] for h in range(PIECES)]
        for h in range(PIECES):
            p1l[h].wait_recv()
            sy = along(mine, 1)[:, h * W:(h + 1) * W]
            for k in reversed(range(1, Q)):
                q2 = lax.rem(q + k, Q)
                encode(
                    ql.at[h, k - 1], al[h, c, q2] + r1l[h, q2] - wide(cols[1, q2], W) * sy
                )
                copy = remote(
                    ql.at[h, k - 1], rl.at[h, k - 1], s2l.at[h, k - 1], e2l.at[h, k - 1],
                    {"tm": 2 * q2 + c},
                )
                copy.start()
                p2l[h].append(copy)
            al[h, c, q] = al[h, c, q] + r1l[h, q] - wide(cols[1, q], W) * sy

    count_f = wide(number, F)

    def to_groups(buf, send, recv):
        out = []
        for k in range(1, G):
            out.append(remote(
                buf.at[z], buf.at[z], send.at[k - 1], recv.at[k - 1], {"group": lax.rem(z + k, G)}
            ))
            out[-1].start()
        return out

    def from_groups(buf, send, recv):
        for k in range(1, G):
            slot = lax.rem(z + G - k, G)
            remote(
                buf.at[slot], buf.at[slot], send.at[k - 1], recv.at[k - 1], {"group": slot}
            ).wait_recv()

    with jax.named_scope("t_zi"):
        for copy in p2i:
            copy.wait_recv()
        total = ai[c, q] + fix[0]
        for k in ((2,) if square else range(Q - 1)):
            total = total + decode(ri.at[k])
        encode(zi.at[z], total)
        zi_copies = to_groups(zi, szi, ezi)
        gi_ref[...] = total / count_f

    zl_copies = []
    for h in range(PIECES):
        with jax.named_scope("t_p2l"):
            for copy in p2l[h]:
                copy.wait_recv()
            part = slice(h * W, (h + 1) * W)
            total = al[h, c, q] + fix[1, :, part]
            for k in range(Q - 1):
                total = total + decode(rl.at[h, k])
            encode(zl.at[h, z], total)
            zl_copies.append(to_groups(zl.at[h], szl.at[h], ezl.at[h]))
            gl_ref[:, part] = total / count_f[:, part]

    with jax.named_scope("t_pool"):
        from_groups(s_grp, ssz, esz)
        everyone = s_grp[0]
        for k in range(1, G):
            everyone = everyone + s_grp[k]
        s_mate[...] = everyone[0:2 * FR]
        whole = everyone[2 * FR:2 * FR + 1]
        for kind in range(2):
            term = -outer(s_mate, kind, 1.0 / whole)
            for k in range(G):
                term = term + outer(s_grp.at[k], kind, 1.0 / s_grp[k, 2 * FR:2 * FR + 1, :])
            fix[kind] = term
        whole_f = wide(whole, F)

    with jax.named_scope("t_zi_in"):
        from_groups(zi, szi, ezi)
        total = fix[0]
        for k in range(G):
            total = total + decode(zi.at[k])
        pi_ref[...] = total / whole_f
    for h in range(PIECES):
        with jax.named_scope("t_zl_in"):
            from_groups(zl.at[h], szl.at[h], ezl.at[h])
            part = slice(h * W, (h + 1) * W)
            total = fix[1, :, part]
            for k in range(G):
                total = total + decode(zl.at[h, k])
            po_ref[:, part] = total / whole_f[:, part]

    with jax.named_scope("t_end"):
        sent(lambda copy: copy.wait_send())
        if square:
            over.wait_send()
        for group in [[p1i, mate], chips, groups, p1l, p2i, *p2l, zi_copies, *zl_copies]:
            for copy in group:
                copy.wait_send()


def place(gi, gl, pi, po, gi_out, gl_out, pi_out, po_out):
    gi_out[0] = gi[...]
    gl_out[0] = gl[...]
    pi_out[...] = pi[...]
    po_out[...] = po[...]


def on_device(T, G, frames, pair_count):
    _, R, F = frames.shape
    S, Q, H, W = F // T, T // 2, LAG // CUTS, F // PIECES
    NB = R // H
    FR = F // LANES
    f32, bf16, i16 = jnp.float32, jnp.bfloat16, jnp.int16
    V, D = pltpu.VMEM, pltpu.SemaphoreType.DMA
    vmem = pl.BlockSpec(memory_space=pltpu.VMEM)
    n = max(Q - 1, 3)
    results = pl.pallas_call(
        functools.partial(kernel, T, G),
        out_shape=(jax.ShapeDtypeStruct((S, F), f32),) * 4,
        in_specs=[pl.BlockSpec(memory_space=pltpu.SMEM), pl.BlockSpec(memory_space=pl.ANY)],
        out_specs=(vmem,) * 4,
        scratch_shapes=[
            V((NB, H, F), bf16),
            V((NB, F + PAD, H), bf16),
            V((CUTS, H, F), bf16),
            V((CUTS, H, F), bf16),
            V((F + PAD, F), f32),
            V((2, Q, S, F), f32),
            V((PIECES, 2, Q, S, W), f32),
            V((Q, S, F), f32),
            V((PIECES, Q, S, W), f32),
            V((n, S + PAD, F), i16),
            V((n, S + PAD, F), i16),
            V((PIECES, Q - 1, S + PAD, W), i16),
            V((PIECES, Q - 1, S + PAD, W), i16),
            V((G, S + PAD, F), i16),
            V((PIECES, G, S + PAD, W), i16),
            V((2 * FR, LANES), f32),
            V((2 * FR, LANES), f32),
            V((Q, 2 * FR, LANES), f32),
            V((G, 2 * FR + 8, LANES), f32),
            V((2, Q, S, LANES), f32),
            V((2, S, F), f32),
            D((NB,)),
            D((2, CUTS)),
            D((2, CUTS)),
            D((1 + PIECES,)),
            D((1 + PIECES,)),
            D((n,)),
            D((n,)),
            D((PIECES, Q - 1)),
            D((PIECES, Q - 1)),
            D((G - 1,)),
            D((G - 1,)),
            D((PIECES, G - 1)),
            D((PIECES, G - 1)),
            D((1,)),
            D((1,)),
            D((Q - 1,)),
            D((Q - 1,)),
            D((G - 1,)),
            D((G - 1,)),
        ],
        compiler_params=pltpu.CompilerParams(
            collective_id=0, has_side_effects=True, vmem_limit_bytes=48 * 1024 * 1024
        ),
    )(pair_count, frames)
    return pl.pallas_call(
        place,
        out_shape=(
            jax.ShapeDtypeStruct((1, S, F), f32),
            jax.ShapeDtypeStruct((1, S, F), f32),
            jax.ShapeDtypeStruct((S, F), f32),
            jax.ShapeDtypeStruct((S, F), f32),
        ),
        in_specs=[vmem] * 4,
        out_specs=(vmem,) * 4,
        compiler_params=pltpu.CompilerParams(vmem_limit_bytes=4 * 1024 * 1024),
    )(*results)


def solution(mesh):
    in_specs = (P("group", "tm", None), P("group"))
    out_specs = (P("group", "tm", None), P("group", "tm", None), P("tm", None), P("tm", None))
    body = functools.partial(on_device, mesh.shape["tm"], mesh.shape["group"])
    return jax.shard_map(
        body, mesh=mesh, in_specs=in_specs, out_specs=out_specs, check_vma=False
    )
```

```python
import functools

import jax
import jax.numpy as jnp
from jax import lax
from jax.experimental import pallas as pl
from jax.experimental.pallas import tpu as pltpu
from jax.sharding import PartitionSpec as P

LAG = 2048
MESH = pl.DeviceIdType.MESH
PAD = 16
CUTS = 4
PIECES = 2
LANES = 128
LEVELS = 32700.0
STEPS = 8.0
LEAST = 1e-30
LOAD = 4


def code_rows(S, W):
    return W // LANES * S + PAD


def encode(ref, block):
    S, W = block.shape
    top = jnp.maximum(jnp.max(jnp.abs(block), axis=0, keepdims=True), LEAST)
    power = jnp.ceil(STEPS * jnp.log2(top * (1.0 / LEVELS)))
    codes = jnp.round(block * (1.0 / jnp.exp2(power * (1.0 / STEPS)))).astype(jnp.int32)
    groups = W // LANES
    for g in range(groups):
        ref[g * S:(g + 1) * S, :] = codes[:, g * LANES:(g + 1) * LANES].astype(jnp.int16)
    row = lax.broadcasted_iota(jnp.int32, (PAD, LANES), 0)
    powers = jnp.zeros((PAD, LANES), jnp.float32)
    for g in range(groups):
        part = jnp.broadcast_to(power[:, g * LANES:(g + 1) * LANES], (PAD, LANES))
        powers = jnp.where(row == g, part, powers)
    ref[groups * S:, :] = powers.astype(jnp.int32).astype(jnp.int16)


def decode(ref, S):
    groups = (ref.shape[0] - PAD) // S
    powers = ref[groups * S:, :].astype(jnp.int32).astype(jnp.float32)
    units = jnp.exp2(powers * (1.0 / STEPS))
    parts = [
        ref[g * S:(g + 1) * S, :].astype(jnp.int32).astype(jnp.float32) * units[g:g + 1]
        for g in range(groups)
    ]
    return parts[0] if groups == 1 else jnp.concatenate(parts, axis=1)


def wide(column, width):
    return jnp.concatenate([column] * (width // LANES), axis=1)


def kernel(
    T, G, count_ref, frames_ref, gi_ref, gl_ref, pi_ref, po_ref,
    x, xt, head, tail, acc, ai, al, r1i, r1l, qi, ri, ql, rl, zi, zs, zl, zh, za,
    s_own, s_mate, s_chip, s_grp, cols, fix,
    ld, nears, nearr, hs, hr, s1, e1, s2, e2, sz, ez, ss, es,
):
    F = frames_ref.shape[2]
    R = frames_ref.shape[1]
    H = LAG // CUTS
    NB = R // H
    W = F // PIECES
    S = F // T
    Q = T // 2
    FR = F // LANES
    NEAR = CUTS // 2
    f32 = jnp.float32
    me = lax.axis_index("tm")
    z = lax.axis_index("group")
    c = lax.rem(me, 2)
    q = lax.div(me, 2)
    partner = me + 1 - 2 * c
    count = count_ref[0]

    def remote(src, dst, a, b, dev):
        return pltpu.make_async_remote_copy(
            src_ref=src, dst_ref=dst, send_sem=a, recv_sem=b,
            device_id=dev, device_id_type=MESH,
        )

    def load(i):
        return pltpu.make_async_copy(
            frames_ref.at[0, pl.ds(i * LOAD * H, LOAD * H)], x.at[pl.ds(i * LOAD * H, LOAD * H)], ld.at[i]
        )

    def block(j):
        return x[pl.ds(pl.multiple_of(j * H, H), H), :]

    for i in range(NB // LOAD):
        load(i).start()

    barrier = pltpu.get_barrier_semaphore()
    for k in range(1, T):
        pl.semaphore_signal(
            barrier, inc=1, device_id={"tm": lax.rem(me + k, T)}, device_id_type=MESH
        )
    for k in range(1, G):
        pl.semaphore_signal(
            barrier, inc=1, device_id={"group": lax.rem(z + k, G)}, device_id_type=MESH
        )
    with jax.named_scope("t_barrier"):
        pl.semaphore_wait(barrier, T - 1 + G - 1)

    def kept(b):
        if T != 8:
            return CUTS // 2
        turn = lax.rem(b, 2) * (1 - lax.rem(lax.div(b, 2), 2))
        return CUTS // 2 + turn * (2 * lax.div(b, 4) - 1)

    before = lax.rem(me + T - 1, T)

    near_head = remote(
        frames_ref.at[0, pl.ds(0, NEAR * H)], head.at[pl.ds(0, NEAR * H)],
        nears.at[0], nearr.at[0], {"tm": partner},
    )
    near_tail = remote(
        frames_ref.at[0, pl.ds(R - LAG + NEAR * H, (CUTS - NEAR) * H)],
        tail.at[pl.ds(NEAR * H, (CUTS - NEAR) * H)],
        nears.at[0], nearr.at[0], {"tm": partner},
    )

    def send_head(j):
        return remote(
            frames_ref.at[0, pl.ds(j * H, H)], head.at[pl.ds(j * H, H)], hs.at[j], hr.at[j],
            {"tm": me - 1},
        )

    def send_tail(j):
        return remote(
            frames_ref.at[0, pl.ds(R - LAG + j * H, H)], tail.at[pl.ds(j * H, H)], hs.at[j], hr.at[j],
            {"tm": me + 1},
        )

    def far(act, now):
        for j in range(CUTS):
            @pl.when((me > 0) & (c == 0) & (j < kept(before)) & now(kept(before) < NEAR))
            def _():
                act(send_head(j))

            @pl.when((me < T - 1) & (c == 1) & (j >= kept(me)) & now(kept(me) > NEAR))
            def _():
                act(send_tail(j))

    def sent(act):
        pl.when(c == 0)(lambda: act(near_tail))
        pl.when(c == 1)(lambda: act(near_head))

    far(lambda copy: copy.start(), jnp.logical_not)
    sent(lambda copy: copy.start())

    def put_transposed(block, base, slot):
        rows = lax.broadcasted_iota(jnp.int32, (H, LANES), 0) + base
        keep = jnp.where(rows < count, 1.0, 0.0).astype(jnp.bfloat16)
        xt[slot, 0:F, :] = (block * wide(keep, F)).T

    def put_masks(base, slot):
        frame = lax.broadcasted_iota(jnp.int32, (PAD, H), 1) + base
        kind = lax.broadcasted_iota(jnp.int32, (PAD, H), 0)
        first = jnp.where(kind == 0, 0, LAG)
        valid = (frame >= first) & (frame < first + count) & (kind < 2)
        xt[slot, F:, :] = jnp.where(valid, 1.0, 0.0).astype(jnp.bfloat16)

    def product(slot, block):
        return jnp.dot(xt[slot, 0:F, :], block, preferred_element_type=f32)

    acc[...] = jnp.zeros_like(acc)

    def inst_step(i, carry):
        @pl.when(lax.rem(2 * i, LOAD) == 0)
        def _():
            load(lax.div(2 * i, LOAD)).wait()

        for j in (2 * i, 2 * i + 1):
            put_transposed(block(j), me * R + j * H, j)
            put_masks(me * R + j * H, j)
        acc[...] += (
            jnp.dot(xt[2 * i], block(2 * i), preferred_element_type=f32)
            + jnp.dot(xt[2 * i + 1], block(2 * i + 1), preferred_element_type=f32)
        )
        return carry

    with jax.named_scope("t_inst"):
        lax.fori_loop(0, NB // 2, inst_step, 0)
    for d in range(T):
        ai[d % 2, d // 2] = acc[d * S:(d + 1) * S, :]
    for k in range(2):
        for j in range(FR):
            s_own[k * FR + j:k * FR + j + 1, :] = acc[F + k:F + k + 1, j * LANES:(j + 1) * LANES]
    p1i = remote(ai.at[1 - c], r1i, s1.at[0], e1.at[0], {"tm": partner})
    p1i.start()
    mate = remote(s_own, s_mate, ss.at[0], es.at[0], {"tm": partner})
    mate.start()

    acc[...] = jnp.zeros_like(acc)

    def lag_step(i, carry):
        j = 2 * i
        acc[0:F, :] += product(j, block(j + CUTS)) + product(j + 1, block(j + 1 + CUTS))
        return carry

    with jax.named_scope("t_lag"):
        lax.fori_loop(0, (NB - CUTS) // 2, lag_step, 0)
    far(lambda copy: copy.start(), lambda late: late)

    def clip(v, top):
        return jnp.minimum(jnp.maximum(v, 0), top)

    def vector(n):
        return jnp.broadcast_to(n, (1, LANES)).astype(f32)

    def weights(chip):
        a = chip * 2 * R
        nx = clip(count - a, 2 * R)
        ny = clip(count + LAG - a, 2 * R) - clip(LAG - a, 2 * R)
        low = jnp.where(chip > 0, kept(2 * chip - 1) * H - LAG, 0)
        high = jnp.where(chip < Q - 1, kept(2 * chip + 1) * H - LAG, 0)
        pairs = clip(count - a - low, 2 * R + high - low)
        vx, vy = vector(jnp.maximum(nx, 1)), vector(jnp.maximum(ny, 1))
        return 1.0 / vx, vector(pairs) / (vx * vy)

    lanes = lax.broadcasted_iota(jnp.int32, (S, LANES), 1)
    rows = lax.broadcasted_iota(jnp.int32, (S, LANES), 0)

    def upright(row, offset):
        picked = jnp.where(lanes == rows + offset, jnp.broadcast_to(row, (S, LANES)), 0.0)
        return jnp.broadcast_to(jnp.sum(picked, axis=1, keepdims=True), (S, LANES))

    def along(ref, kind):
        return jnp.concatenate([ref[kind * FR + j:kind * FR + j + 1, :] for j in range(FR)], axis=1)

    class Group:
        def __init__(self, a, b, like, n):
            self.pairs, self.a, self.b, self.like, self.n = [], a, b, like, n

        def send(self, src, dst, dev):
            remote(src, dst, self.a, self.b, dev).start()

        def whole(self):
            ref = self.like.at[pl.ds(0, self.n)]
            return remote(ref, ref, self.a, self.b, {"tm": partner})

        def wait_recv(self):
            self.whole().wait_recv()

        def wait_send(self):
            self.whole().wait_send()

    with jax.named_scope("t_p1i"):
        mate.wait_recv()
        s_chip[q] = s_own[...] + s_mate[...]
        chips = Group(ss.at[1], es.at[1], s_chip, Q - 1)
        for k in range(1, Q):
            chips.send(s_chip.at[q], s_chip.at[q], {"tm": 2 * lax.rem(q + k, Q) + c})
        wx, wl = weights(q)
        mine = s_chip.at[q]
        for k in range(Q):
            at = 2 * k * S
            col = upright(mine[at // LANES:at // LANES + 1, :], at % LANES + c * S)
            cols[0, k] = col * wx
            cols[1, k] = col * wl
        p1i.wait_recv()
        sx = along(mine, 0)
        for k in range(Q):
            ai[c, k] = ai[c, k] + r1i[k] - wide(cols[0, k], F) * sx

    square = Q == 4
    with jax.named_scope("t_inst_send"):
        if square:
            side, level = lax.rem(q, 2), lax.div(q, 2)
            across = q + 1 - 2 * side
            for k in range(2):
                encode(qi.at[k], ai[c, 2 - 2 * level + k])
            over = remote(
                qi.at[pl.ds(0, 2)], ri.at[pl.ds(0, 2)], s2.at[0], e2.at[0],
                {"tm": 2 * lax.rem(q + 2, Q) + c},
            )
            over.start()
            p2i = remote(qi.at[2], ri.at[2], s2.at[1], e2.at[1], {"tm": 2 * across + c})
        else:
            p2i = Group(s2.at[1], e2.at[1], ri, Q - 1)
            for k in range(1, Q):
                q2 = lax.rem(q + k, Q)
                encode(qi.at[k - 1], ai[c, q2])
                p2i.send(qi.at[k - 1], ri.at[k - 1], {"tm": 2 * q2 + c})

    def take_head(j):
        acc[0:F, :] += product(NB - CUTS + j, head[pl.ds(pl.multiple_of(j * H, H), H), :])

    def take_tail(j):
        put_transposed(tail[pl.ds(pl.multiple_of(j * H, H), H), :], me * R - LAG + j * H, j)
        acc[0:F, :] += product(j, block(j))

    def near_heads():
        near_head.wait_recv()

        def step(j, carry):
            take_head(j)
            return carry

        lax.fori_loop(0, NEAR, step, 0)

    def near_tails():
        near_tail.wait_recv()

        def step(j, carry):
            take_tail(j)
            return carry

        lax.fori_loop(NEAR, CUTS, step, 0)

    def far_heads():
        def step(j, carry):
            send_head(j).wait_recv()
            take_head(j)
            return carry

        lax.fori_loop(0, kept(me), step, 0)

    def far_tails():
        def step(j, carry):
            send_tail(j).wait_recv()
            take_tail(j)
            return carry

        lax.fori_loop(kept(before), CUTS, step, 0)

    with jax.named_scope("t_halo_near"):
        pl.when(c == 0)(near_heads)
        pl.when(c == 1)(near_tails)
    with jax.named_scope("t_halo_far"):
        pl.when((me < T - 1) & (c == 1))(far_heads)
        pl.when((me > 0) & (c == 0))(far_tails)

    with jax.named_scope("t_lag_out"):
        p1l = []
        for h in range(PIECES):
            for d in range(T):
                al[h, d % 2, d // 2] = acc[d * S:(d + 1) * S, h * W:(h + 1) * W]
            p1l.append(
                remote(al.at[h, 1 - c], r1l.at[h], s1.at[1 + h], e1.at[1 + h], {"tm": partner})
            )
            p1l[h].start()

    with jax.named_scope("t_sums"):
        chips.wait_recv()

        at = lax.div(me * S, LANES)
        off = lax.rem(me * S, LANES)

        def outer(ref, kind, scale):
            return wide(upright(ref[pl.ds(at, 1), :], off) * scale, F) * along(ref, kind)

        total = s_chip[0]
        for k in range(1, Q):
            total = total + s_chip[k]
        s_grp[z, 0:2 * FR, :] = total
        s_grp[z, 2 * FR:, :] = jnp.broadcast_to(vector(count), (8, LANES))
        groups = Group(ss.at[2], es.at[2], s_grp, G - 1)
        for k in range(1, G):
            groups.send(s_grp.at[z], s_grp.at[z], {"group": lax.rem(z + k, G)})
        number = vector(count)
        for kind in range(2):
            term = -outer(s_grp.at[z], kind, 1.0 / number)
            for k in range(Q):
                term = term + outer(s_chip.at[k], kind, weights(k)[kind])
            fix[kind] = term
        count_f = wide(number, F)

    with jax.named_scope("t_inst_x"):
        if square:
            over.wait_recv()
            for k in range(2):
                ai[c, 2 * level + k] += decode(ri.at[k], S)
            encode(qi.at[2], ai[c, across])
            p2i.start()

    with jax.named_scope("t_p1l"):
        p2l = []
        for h in range(PIECES):
            p1l[h].wait_recv()
            sy = along(mine, 1)[:, h * W:(h + 1) * W]
            p2l.append(Group(s2.at[2 + h], e2.at[2 + h], rl.at[h], Q - 1))
            for k in reversed(range(1, Q)):
                q2 = lax.rem(q + k, Q)
                encode(
                    ql.at[h, k - 1], al[h, c, q2] + r1l[h, q2] - wide(cols[1, q2], W) * sy
                )
                p2l[h].send(ql.at[h, k - 1], rl.at[h, k - 1], {"tm": 2 * q2 + c})
            al[h, c, q] = al[h, c, q] + r1l[h, q] - wide(cols[1, q], W) * sy

    def to_groups(group, buf):
        for k in range(1, G):
            group.send(buf.at[z], buf.at[z], {"group": lax.rem(z + k, G)})

    shares = G if F % (G * LANES) == 0 else 1
    N = F // shares
    with jax.named_scope("t_zi"):
        p2i.wait_recv()
        total = ai[c, q] + fix[0]
        for k in ((2,) if square else range(Q - 1)):
            total = total + decode(ri.at[k], S)
        gi_ref[...] = total / count_f
        part_sums = Group(sz.at[0], ez.at[0], zs, G - 1)
        full_sums = Group(sz.at[1], ez.at[1], zi, G - 1)
        if shares == G:
            for w in range(G):
                cut = total[:, w * N:(w + 1) * N]

                @pl.when(w != z)
                def _():
                    encode(zi.at[w], cut)
                    part_sums.send(zi.at[w], zs.at[z], {"group": w})

                @pl.when(w == z)
                def _():
                    ai[c, q, :, 0:N] = cut
        else:
            encode(zi.at[z], total)
            to_groups(full_sums, zi)

    hub = G == 4
    zl_groups = []

    def lag_session(h):
        with jax.named_scope("t_p2l"):
            p2l[h].wait_recv()
            part = slice(h * W, (h + 1) * W)
            total = al[h, c, q] + fix[1, :, part]
            for k in range(Q - 1):
                total = total + decode(rl.at[h, k], S)
            gl_ref[:, part] = total / count_f[:, part]
            encode(zl.at[h, z], total)
            zl_groups.append(Group(sz.at[2 + h], ez.at[2 + h], zl.at[h], G - 1))
            to_groups(zl_groups[h], zl.at[h])

    for h in range(PIECES):
        lag_session(h)

    if shares == G:
        with jax.named_scope("t_zi_share"):
            part_sums.wait_recv()
            total = ai[c, q, :, 0:N]
            for k in range(1, G):
                total = total + decode(zs.at[lax.rem(z + k, G)], S)
            encode(za.at[z], total)
            full_sums = Group(sz.at[1], ez.at[1], za, G - 1)
            to_groups(full_sums, za)

    with jax.named_scope("t_pool"):
        groups.wait_recv()
        everyone = s_grp[0]
        for k in range(1, G):
            everyone = everyone + s_grp[k]
        s_mate[...] = everyone[0:2 * FR]
        all_n = everyone[2 * FR:2 * FR + 1]
        for kind in range(2):
            term = -outer(s_mate, kind, 1.0 / all_n)
            for k in range(G):
                term = term + outer(s_grp.at[k], kind, 1.0 / s_grp[k, 2 * FR:2 * FR + 1, :])
            fix[kind] = term
        whole_f = wide(all_n, F)

    for h in range(PIECES):
        with jax.named_scope("t_zl_in"):
            zl_groups[h].wait_recv()
            part = slice(h * W, (h + 1) * W)
            total = fix[1, :, part]
            for k in range(G):
                total = total + decode(zl.at[h, k], S)
            po_ref[:, part] = total / whole_f[:, part]

    with jax.named_scope("t_zi_in"):
        full_sums.wait_recv()
        if shares == G:
            for w in range(G):
                part = slice(w * N, (w + 1) * N)
                pi_ref[:, part] = (fix[0, :, part] + decode(za.at[w], S)) / whole_f[:, part]
        else:
            total = fix[0]
            for k in range(G):
                total = total + decode(zi.at[k], S)
            pi_ref[...] = total / whole_f

    with jax.named_scope("t_end"):
        sent(lambda copy: copy.wait_send())
        far(lambda copy: copy.wait_send(), lambda late: late)
        far(lambda copy: copy.wait_send(), jnp.logical_not)
        if square:
            over.wait_send()
        if shares == G:
            part_sums.wait_send()
        for copy in [p1i, mate, chips, groups, *p1l, p2i, *p2l, full_sums, *zl_groups]:
            copy.wait_send()


def place(gi, gl, pi, po, gi_out, gl_out, pi_out, po_out):
    gi_out[0] = gi[...]
    gl_out[0] = gl[...]
    pi_out[...] = pi[...]
    po_out[...] = po[...]


def on_device(T, G, frames, pair_count):
    _, R, F = frames.shape
    S, Q, H, W = F // T, T // 2, LAG // CUTS, F // PIECES
    NB = R // H
    FR = F // LANES
    f32, bf16, i16 = jnp.float32, jnp.bfloat16, jnp.int16
    V, D = pltpu.VMEM, pltpu.SemaphoreType.DMA
    vmem = pl.BlockSpec(memory_space=pltpu.VMEM)
    n = max(Q - 1, 3)
    N = F // G if F % (G * LANES) == 0 else F
    results = pl.pallas_call(
        functools.partial(kernel, T, G),
        out_shape=(jax.ShapeDtypeStruct((S, F), f32),) * 4,
        in_specs=[pl.BlockSpec(memory_space=pltpu.SMEM), pl.BlockSpec(memory_space=pl.ANY)],
        out_specs=(vmem,) * 4,
        scratch_shapes=[
            V((R, F), bf16),
            V((NB, F + PAD, H), bf16),
            V((LAG, F), bf16),
            V((LAG, F), bf16),
            V((F + PAD, F), f32),
            V((2, Q, S, F), f32),
            V((PIECES, 2, Q, S, W), f32),
            V((Q, S, F), f32),
            V((PIECES, Q, S, W), f32),
            V((n, code_rows(S, F), LANES), i16),
            V((n, code_rows(S, F), LANES), i16),
            V((PIECES, Q - 1, code_rows(S, W), LANES), i16),
            V((PIECES, Q - 1, code_rows(S, W), LANES), i16),
            V((G, code_rows(S, N), LANES), i16),
            V((G, code_rows(S, N), LANES), i16),
            V((PIECES, G, code_rows(S, W), LANES), i16),
            V((PIECES, code_rows(S, W), LANES), i16),
            V((G, code_rows(S, N), LANES), i16),
            V((2 * FR, LANES), f32),
            V((2 * FR, LANES), f32),
            V((Q, 2 * FR, LANES), f32),
            V((G, 2 * FR + 8, LANES), f32),
            V((2, Q, S, LANES), f32),
            V((2, S, F), f32),
            D((NB // LOAD,)),
            D((1,)),
            D((1,)),
            D((CUTS,)),
            D((CUTS,)),
            D((1 + PIECES,)),
            D((1 + PIECES,)),
            D((2 + PIECES,)),
            D((2 + PIECES,)),
            D((2 + PIECES,)),
            D((2 + PIECES,)),
            D((3,)),
            D((3,)),
        ],
        compiler_params=pltpu.CompilerParams(
            collective_id=0, has_side_effects=True, vmem_limit_bytes=48 * 1024 * 1024
        ),
    )(pair_count, frames)
    return pl.pallas_call(
        place,
        out_shape=(
            jax.ShapeDtypeStruct((1, S, F), f32),
            jax.ShapeDtypeStruct((1, S, F), f32),
            jax.ShapeDtypeStruct((S, F), f32),
            jax.ShapeDtypeStruct((S, F), f32),
        ),
        in_specs=[vmem] * 4,
        out_specs=(vmem,) * 4,
        compiler_params=pltpu.CompilerParams(vmem_limit_bytes=4 * 1024 * 1024),
    )(*results)


def solution(mesh):
    in_specs = (P("group", "tm", None), P("group"))
    out_specs = (P("group", "tm", None), P("group", "tm", None), P("tm", None), P("tm", None))
    body = functools.partial(on_device, mesh.shape["tm"], mesh.shape["group"])
    return jax.shard_map(
        body, mesh=mesh, in_specs=in_specs, out_specs=out_specs, check_vma=False
    )
```

```python
import functools

import jax
import jax.numpy as jnp
from jax import lax
from jax.experimental import pallas as pl
from jax.experimental.pallas import tpu as pltpu
from jax.sharding import PartitionSpec as P

LAG = 2048
MESH = pl.DeviceIdType.MESH
PAD = 16
CUTS = 4
PIECES = 2
LANES = 128
LEVELS = 32700.0
STEPS = 8.0
LEAST = 1e-30
LOAD = 4


def code_rows(S, W):
    return W // LANES * S + PAD


def encode(ref, block):
    S, W = block.shape
    top = jnp.maximum(jnp.max(jnp.abs(block), axis=0, keepdims=True), LEAST)
    power = jnp.ceil(STEPS * jnp.log2(top * (1.0 / LEVELS)))
    codes = jnp.round(block * (1.0 / jnp.exp2(power * (1.0 / STEPS)))).astype(jnp.int32)
    groups = W // LANES
    for g in range(groups):
        ref[g * S:(g + 1) * S, :] = codes[:, g * LANES:(g + 1) * LANES].astype(jnp.int16)
    row = lax.broadcasted_iota(jnp.int32, (PAD, LANES), 0)
    powers = jnp.zeros((PAD, LANES), jnp.float32)
    for g in range(groups):
        part = jnp.broadcast_to(power[:, g * LANES:(g + 1) * LANES], (PAD, LANES))
        powers = jnp.where(row == g, part, powers)
    ref[groups * S:, :] = powers.astype(jnp.int32).astype(jnp.int16)


def decode(ref, S):
    groups = (ref.shape[0] - PAD) // S
    powers = ref[groups * S:, :].astype(jnp.int32).astype(jnp.float32)
    units = jnp.exp2(powers * (1.0 / STEPS))
    parts = [
        ref[g * S:(g + 1) * S, :].astype(jnp.int32).astype(jnp.float32) * units[g:g + 1]
        for g in range(groups)
    ]
    return parts[0] if groups == 1 else jnp.concatenate(parts, axis=1)


def wide(column, width):
    return jnp.concatenate([column] * (width // LANES), axis=1)


def kernel(
    T, G, count_ref, frames_ref, gi_ref, gl_ref, pi_ref, po_ref,
    x, xt, head, tail, acc, ai, al, r1i, r1l, qi, ri, ql, rl, zi, zs, zl, zh, za, zg,
    s_own, s_mate, s_chip, s_grp, cols, fix,
    ld, nears, nearr, hs, hr, s1, e1, s2, e2, sz, ez, ss, es,
):
    F = frames_ref.shape[2]
    R = frames_ref.shape[1]
    H = LAG // CUTS
    NB = R // H
    W = F // PIECES
    S = F // T
    Q = T // 2
    FR = F // LANES
    NEAR = CUTS // 2
    f32 = jnp.float32
    me = lax.axis_index("tm")
    z = lax.axis_index("group")
    c = lax.rem(me, 2)
    q = lax.div(me, 2)
    partner = me + 1 - 2 * c
    count = count_ref[0]

    def remote(src, dst, a, b, dev):
        return pltpu.make_async_remote_copy(
            src_ref=src, dst_ref=dst, send_sem=a, recv_sem=b,
            device_id=dev, device_id_type=MESH,
        )

    def load(i):
        return pltpu.make_async_copy(
            frames_ref.at[0, pl.ds(i * LOAD * H, LOAD * H)], x.at[pl.ds(i * LOAD * H, LOAD * H)], ld.at[i]
        )

    def block(j):
        return x[pl.ds(pl.multiple_of(j * H, H), H), :]

    for i in range(NB // LOAD):
        load(i).start()

    barrier = pltpu.get_barrier_semaphore()
    for k in range(1, T):
        pl.semaphore_signal(
            barrier, inc=1, device_id={"tm": lax.rem(me + k, T)}, device_id_type=MESH
        )
    for k in range(1, G):
        pl.semaphore_signal(
            barrier, inc=1, device_id={"group": lax.rem(z + k, G)}, device_id_type=MESH
        )
    with jax.named_scope("t_barrier"):
        pl.semaphore_wait(barrier, T - 1 + G - 1)

    def kept(b):
        if T != 8:
            return CUTS // 2
        turn = lax.rem(b, 2) * (1 - lax.rem(lax.div(b, 2), 2))
        return CUTS // 2 + turn * (2 * lax.div(b, 4) - 1)

    before = lax.rem(me + T - 1, T)

    near_head = remote(
        frames_ref.at[0, pl.ds(0, NEAR * H)], head.at[pl.ds(0, NEAR * H)],
        nears.at[0], nearr.at[0], {"tm": partner},
    )
    near_tail = remote(
        frames_ref.at[0, pl.ds(R - LAG + NEAR * H, (CUTS - NEAR) * H)],
        tail.at[pl.ds(NEAR * H, (CUTS - NEAR) * H)],
        nears.at[0], nearr.at[0], {"tm": partner},
    )

    def send_head(j):
        return remote(
            frames_ref.at[0, pl.ds(j * H, H)], head.at[pl.ds(j * H, H)], hs.at[j], hr.at[j],
            {"tm": me - 1},
        )

    def send_tail(j):
        return remote(
            frames_ref.at[0, pl.ds(R - LAG + j * H, H)], tail.at[pl.ds(j * H, H)], hs.at[j], hr.at[j],
            {"tm": me + 1},
        )

    def far(act, now):
        for j in range(CUTS):
            @pl.when((me > 0) & (c == 0) & (j < kept(before)) & now(kept(before) < NEAR))
            def _():
                act(send_head(j))

            @pl.when((me < T - 1) & (c == 1) & (j >= kept(me)) & now(kept(me) > NEAR))
            def _():
                act(send_tail(j))

    def sent(act):
        pl.when(c == 0)(lambda: act(near_tail))
        pl.when(c == 1)(lambda: act(near_head))

    far(lambda copy: copy.start(), jnp.logical_not)
    sent(lambda copy: copy.start())

    def put_transposed(block, base, slot):
        rows = lax.broadcasted_iota(jnp.int32, (H, LANES), 0) + base
        keep = jnp.where(rows < count, 1.0, 0.0).astype(jnp.bfloat16)
        xt[slot, 0:F, :] = (block * wide(keep, F)).T

    def put_masks(base, slot):
        frame = lax.broadcasted_iota(jnp.int32, (PAD, H), 1) + base
        kind = lax.broadcasted_iota(jnp.int32, (PAD, H), 0)
        first = jnp.where(kind == 0, 0, LAG)
        valid = (frame >= first) & (frame < first + count) & (kind < 2)
        xt[slot, F:, :] = jnp.where(valid, 1.0, 0.0).astype(jnp.bfloat16)

    def product(slot, block):
        return jnp.dot(xt[slot, 0:F, :], block, preferred_element_type=f32)

    acc[...] = jnp.zeros_like(acc)

    def inst_step(i, carry):
        @pl.when(lax.rem(2 * i, LOAD) == 0)
        def _():
            load(lax.div(2 * i, LOAD)).wait()

        for j in (2 * i, 2 * i + 1):
            put_transposed(block(j), me * R + j * H, j)
            put_masks(me * R + j * H, j)
        acc[...] += (
            jnp.dot(xt[2 * i], block(2 * i), preferred_element_type=f32)
            + jnp.dot(xt[2 * i + 1], block(2 * i + 1), preferred_element_type=f32)
        )
        return carry

    with jax.named_scope("t_inst"):
        lax.fori_loop(0, NB // 2, inst_step, 0)
    for d in range(T):
        ai[d % 2, d // 2] = acc[d * S:(d + 1) * S, :]
    for k in range(2):
        for j in range(FR):
            s_own[k * FR + j:k * FR + j + 1, :] = acc[F + k:F + k + 1, j * LANES:(j + 1) * LANES]
    p1i = remote(ai.at[1 - c], r1i, s1.at[0], e1.at[0], {"tm": partner})
    p1i.start()
    mate = remote(s_own, s_mate, ss.at[0], es.at[0], {"tm": partner})
    mate.start()

    acc[...] = jnp.zeros_like(acc)

    def lag_step(i, carry):
        j = 2 * i
        acc[0:F, :] += product(j, block(j + CUTS)) + product(j + 1, block(j + 1 + CUTS))
        return carry

    with jax.named_scope("t_lag"):
        lax.fori_loop(0, (NB - CUTS) // 2, lag_step, 0)
    far(lambda copy: copy.start(), lambda late: late)

    def clip(v, top):
        return jnp.minimum(jnp.maximum(v, 0), top)

    def vector(n):
        return jnp.broadcast_to(n, (1, LANES)).astype(f32)

    def weights(chip):
        a = chip * 2 * R
        nx = clip(count - a, 2 * R)
        ny = clip(count + LAG - a, 2 * R) - clip(LAG - a, 2 * R)
        low = jnp.where(chip > 0, kept(2 * chip - 1) * H - LAG, 0)
        high = jnp.where(chip < Q - 1, kept(2 * chip + 1) * H - LAG, 0)
        pairs = clip(count - a - low, 2 * R + high - low)
        vx, vy = vector(jnp.maximum(nx, 1)), vector(jnp.maximum(ny, 1))
        return 1.0 / vx, vector(pairs) / (vx * vy)

    lanes = lax.broadcasted_iota(jnp.int32, (S, LANES), 1)
    rows = lax.broadcasted_iota(jnp.int32, (S, LANES), 0)

    def upright(row, offset):
        picked = jnp.where(lanes == rows + offset, jnp.broadcast_to(row, (S, LANES)), 0.0)
        return jnp.broadcast_to(jnp.sum(picked, axis=1, keepdims=True), (S, LANES))

    def along(ref, kind):
        return jnp.concatenate([ref[kind * FR + j:kind * FR + j + 1, :] for j in range(FR)], axis=1)

    class Group:
        def __init__(self, a, b, like, n):
            self.pairs, self.a, self.b, self.like, self.n = [], a, b, like, n

        def send(self, src, dst, dev):
            remote(src, dst, self.a, self.b, dev).start()

        def whole(self):
            ref = self.like.at[pl.ds(0, self.n)]
            return remote(ref, ref, self.a, self.b, {"tm": partner})

        def wait_recv(self):
            self.whole().wait_recv()

        def wait_send(self):
            self.whole().wait_send()

    with jax.named_scope("t_p1i"):
        mate.wait_recv()
        s_chip[q] = s_own[...] + s_mate[...]
        chips = Group(ss.at[1], es.at[1], s_chip, Q - 1)
        for k in range(1, Q):
            chips.send(s_chip.at[q], s_chip.at[q], {"tm": 2 * lax.rem(q + k, Q) + c})
        wx, wl = weights(q)
        mine = s_chip.at[q]
        for k in range(Q):
            at = 2 * k * S
            col = upright(mine[at // LANES:at // LANES + 1, :], at % LANES + c * S)
            cols[0, k] = col * wx
            cols[1, k] = col * wl
        p1i.wait_recv()
        sx = along(mine, 0)
        for k in range(Q):
            ai[c, k] = ai[c, k] + r1i[k] - wide(cols[0, k], F) * sx

    square = Q == 4
    with jax.named_scope("t_inst_send"):
        if square:
            side, level = lax.rem(q, 2), lax.div(q, 2)
            across = q + 1 - 2 * side
            for k in range(2):
                encode(qi.at[k], ai[c, 2 - 2 * level + k])
            over = remote(
                qi.at[pl.ds(0, 2)], ri.at[pl.ds(0, 2)], s2.at[0], e2.at[0],
                {"tm": 2 * lax.rem(q + 2, Q) + c},
            )
            over.start()
            p2i = remote(qi.at[2], ri.at[2], s2.at[1], e2.at[1], {"tm": 2 * across + c})
        else:
            p2i = Group(s2.at[1], e2.at[1], ri, Q - 1)
            for k in range(1, Q):
                q2 = lax.rem(q + k, Q)
                encode(qi.at[k - 1], ai[c, q2])
                p2i.send(qi.at[k - 1], ri.at[k - 1], {"tm": 2 * q2 + c})

    def take_head(j):
        acc[0:F, :] += product(NB - CUTS + j, head[pl.ds(pl.multiple_of(j * H, H), H), :])

    def take_tail(j):
        put_transposed(tail[pl.ds(pl.multiple_of(j * H, H), H), :], me * R - LAG + j * H, j)
        acc[0:F, :] += product(j, block(j))

    def near_heads():
        near_head.wait_recv()

        def step(j, carry):
            take_head(j)
            return carry

        lax.fori_loop(0, NEAR, step, 0)

    def near_tails():
        near_tail.wait_recv()

        def step(j, carry):
            take_tail(j)
            return carry

        lax.fori_loop(NEAR, CUTS, step, 0)

    def relay_instant():
        over.wait_recv()
        for k in range(2):
            ai[c, 2 * level + k] += decode(ri.at[k], S)
        encode(qi.at[2], ai[c, across])
        p2i.start()

    def far_heads():
        def step(j, carry):
            send_head(j).wait_recv()
            take_head(j)
            return carry

        lax.fori_loop(0, kept(me) - 1, step, 0)
        if square:
            pl.when(kept(me) > 1)(relay_instant)
        step(kept(me) - 1, 0)

    def far_tails():
        def step(j, carry):
            send_tail(j).wait_recv()
            take_tail(j)
            return carry

        lax.fori_loop(kept(before), CUTS - 1, step, 0)
        if square:
            pl.when(kept(before) < CUTS - 1)(relay_instant)
        step(CUTS - 1, 0)

    with jax.named_scope("t_halo_near"):
        pl.when(c == 0)(near_heads)
        pl.when(c == 1)(near_tails)
    with jax.named_scope("t_halo_far"):
        has_heads = (me < T - 1) & (c == 1)
        has_tails = (me > 0) & (c == 0)
        pl.when(has_heads)(far_heads)
        pl.when(has_tails)(far_tails)

    with jax.named_scope("t_lag_out"):
        p1l = []
        for h in range(PIECES):
            for d in range(T):
                al[h, d % 2, d // 2] = acc[d * S:(d + 1) * S, h * W:(h + 1) * W]
            p1l.append(
                remote(al.at[h, 1 - c], r1l.at[h], s1.at[1 + h], e1.at[1 + h], {"tm": partner})
            )
            p1l[h].start()

    with jax.named_scope("t_inst_x"):
        if square:
            early = (has_heads & (kept(me) > 1)) | (has_tails & (kept(before) < CUTS - 1))
            pl.when(jnp.logical_not(early))(relay_instant)

    with jax.named_scope("t_p1l"):
        p2l = [Group(s2.at[2 + h], e2.at[2 + h], rl.at[h], Q - 1) for h in range(PIECES)]

        def spread(h, chip):
            @pl.when(chip != q)
            def _():
                sy = along(mine, 1)[:, h * W:(h + 1) * W]
                encode(
                    ql.at[h, chip], al[h, c, chip] + r1l[h, chip] - wide(cols[1, chip], W) * sy
                )
                p2l[h].send(ql.at[h, chip], rl.at[h, q], {"tm": 2 * chip + c})

        def turn(i, n):
            return jnp.where(c == 0, i, n - 1 - i)

        for h in range(PIECES):
            p1l[h].wait_recv()
            spread(h, turn(0, Q))
        for h in range(PIECES):
            for i in range(1, Q):
                spread(h, turn(i, Q))
            sy = along(mine, 1)[:, h * W:(h + 1) * W]
            al[h, c, q] = al[h, c, q] + r1l[h, q] - wide(cols[1, q], W) * sy

    with jax.named_scope("t_sums"):
        chips.wait_recv()

        at = lax.div(me * S, LANES)
        off = lax.rem(me * S, LANES)

        def outer(ref, kind, scale):
            return wide(upright(ref[pl.ds(at, 1), :], off) * scale, F) * along(ref, kind)

        total = s_chip[0]
        for k in range(1, Q):
            total = total + s_chip[k]
        s_grp[z, 0:2 * FR, :] = total
        s_grp[z, 2 * FR:, :] = jnp.broadcast_to(vector(count), (8, LANES))
        groups = Group(ss.at[2], es.at[2], s_grp, G - 1)
        for k in range(1, G):
            groups.send(s_grp.at[z], s_grp.at[z], {"group": lax.rem(z + k, G)})
        number = vector(count)
        for kind in range(2):
            term = -outer(s_grp.at[z], kind, 1.0 / number)
            for k in range(Q):
                term = term + outer(s_chip.at[k], kind, weights(k)[kind])
            fix[kind] = term
        count_f = wide(number, F)

    def to_groups(group, buf):
        for i in range(G):
            w = jnp.where(c == 0, i, G - 1 - i)

            @pl.when(w != z)
            def _():
                group.send(buf.at[z], buf.at[z], {"group": w})

    shares = G if F % (G * LANES) == 0 else 1
    N = F // shares
    with jax.named_scope("t_zi"):
        p2i.wait_recv()
        total = ai[c, q] + fix[0]
        for k in ((2,) if square else range(Q - 1)):
            total = total + decode(ri.at[k], S)
        gi_ref[...] = total / count_f
        part_sums = Group(sz.at[0], ez.at[0], zs, G - 1)
        full_sums = Group(sz.at[1], ez.at[1], zi, G - 1)
        if shares == G:
            for w in range(G):
                cut = total[:, w * N:(w + 1) * N]

                @pl.when(w != z)
                def _():
                    encode(zi.at[w], cut)
                    part_sums.send(zi.at[w], zs.at[z], {"group": w})

                @pl.when(w == z)
                def _():
                    ai[c, q, :, 0:N] = cut
        else:
            encode(zi.at[z], total)
            to_groups(full_sums, zi)

    hub = G == 4
    zl_groups = []
    if hub:
        inner = (z == 1) | (z == 2)
        slot = jnp.where(z < 2, 0, 1)
        inward = remote(za.at[0], za.at[1], sz.at[2], ez.at[2], {"group": jnp.where(z < 2, 1, 2)})
        outward = Group(sz.at[2], ez.at[4], zh, G - 1)

        def hub_recv(k):
            return remote(zh.at[k], zh.at[k], sz.at[2], ez.at[4 + k], {"tm": partner})

    def lag_session(h):
        with jax.named_scope("t_p2l"):
            p2l[h].wait_recv()
            part = slice(h * W, (h + 1) * W)
            total = al[h, c, q] + fix[1, :, part]
            for k in range(1, Q):
                total = total + decode(rl.at[h, lax.rem(q + k, Q)], S)
            gl_ref[:, part] = total / count_f[:, part]
            if hub and h == 0:
                @pl.when(inner)
                def _():
                    al[0, c, q] = total

                @pl.when(jnp.logical_not(inner))
                def _():
                    encode(za.at[0], total)
                    inward.start()
            else:
                encode(zl.at[h, z], total)
                zl_groups.append(Group(sz.at[2 + h], ez.at[2 + h], zl.at[h], G - 1))
                to_groups(zl_groups[-1], zl.at[h])

    lag_session(0)
    if shares == G:
        with jax.named_scope("t_zi_share"):
            part_sums.wait_recv()
            total = ai[c, q, :, 0:N]
            for k in range(1, G):
                total = total + decode(zs.at[lax.rem(z + k, G)], S)
            encode(zg.at[z], total)
            full_sums = Group(sz.at[1], ez.at[1], zg, G - 1)
            to_groups(full_sums, zg)
    for h in range(1, PIECES):
        lag_session(h)
    if hub:
        with jax.named_scope("t_hub"):
            @pl.when(inner)
            def _():
                inward.wait_recv()
                encode(zh.at[slot], al[0, c, q] + decode(za.at[1], S))
                for w in range(G):
                    @pl.when(w != z)
                    def _():
                        remote(
                            zh.at[slot], zh.at[slot], sz.at[2], ez.at[4 + slot], {"group": w}
                        ).start()

    with jax.named_scope("t_pool"):
        groups.wait_recv()
        everyone = s_grp[0]
        for k in range(1, G):
            everyone = everyone + s_grp[k]
        s_mate[...] = everyone[0:2 * FR]
        all_n = everyone[2 * FR:2 * FR + 1]
        for kind in range(2):
            term = -outer(s_mate, kind, 1.0 / all_n)
            for k in range(G):
                term = term + outer(s_grp.at[k], kind, 1.0 / s_grp[k, 2 * FR:2 * FR + 1, :])
            fix[kind] = term
        whole_f = wide(all_n, F)

    def pooled(h):
        part = slice(h * W, (h + 1) * W)
        total = fix[1, :, part]
        if hub and h == 0:
            for k in range(2):
                total = total + decode(zh.at[k], S)
        else:
            for k in range(G):
                total = total + decode(zl.at[h, k], S)
        po_ref[:, part] = total / whole_f[:, part]

    for h in range(1 if hub else 0, PIECES):
        with jax.named_scope("t_zl_in"):
            zl_groups[h - PIECES].wait_recv()
            pooled(h)
    if hub:
        with jax.named_scope("t_hub_in"):
            for k in range(2):
                pl.when(z != 1 + k)(hub_recv(k).wait_recv)
            pooled(0)

    with jax.named_scope("t_zi_in"):
        full_sums.wait_recv()
        if shares == G:
            for w in range(G):
                part = slice(w * N, (w + 1) * N)
                pi_ref[:, part] = (fix[0, :, part] + decode(zg.at[w], S)) / whole_f[:, part]
        else:
            total = fix[0]
            for k in range(G):
                total = total + decode(zi.at[k], S)
            pi_ref[...] = total / whole_f

    with jax.named_scope("t_end"):
        sent(lambda copy: copy.wait_send())
        far(lambda copy: copy.wait_send(), lambda late: late)
        far(lambda copy: copy.wait_send(), jnp.logical_not)
        if square:
            over.wait_send()
        if shares == G:
            part_sums.wait_send()
        if hub:
            pl.when(inner)(outward.wait_send)
            pl.when(jnp.logical_not(inner))(inward.wait_send)
        for copy in [p1i, mate, chips, groups, *p1l, p2i, *p2l, full_sums, *zl_groups]:
            copy.wait_send()


def place(gi, gl, pi, po, gi_out, gl_out, pi_out, po_out):
    gi_out[0] = gi[...]
    gl_out[0] = gl[...]
    pi_out[...] = pi[...]
    po_out[...] = po[...]


def on_device(T, G, frames, pair_count):
    _, R, F = frames.shape
    S, Q, H, W = F // T, T // 2, LAG // CUTS, F // PIECES
    NB = R // H
    FR = F // LANES
    f32, bf16, i16 = jnp.float32, jnp.bfloat16, jnp.int16
    V, D = pltpu.VMEM, pltpu.SemaphoreType.DMA
    vmem = pl.BlockSpec(memory_space=pltpu.VMEM)
    n = max(Q - 1, 3)
    N = F // G if F % (G * LANES) == 0 else F
    results = pl.pallas_call(
        functools.partial(kernel, T, G),
        out_shape=(jax.ShapeDtypeStruct((S, F), f32),) * 4,
        in_specs=[pl.BlockSpec(memory_space=pltpu.SMEM), pl.BlockSpec(memory_space=pl.ANY)],
        out_specs=(vmem,) * 4,
        scratch_shapes=[
            V((R, F), bf16),
            V((NB, F + PAD, H), bf16),
            V((LAG, F), bf16),
            V((LAG, F), bf16),
            V((F + PAD, F), f32),
            V((2, Q, S, F), f32),
            V((PIECES, 2, Q, S, W), f32),
            V((Q, S, F), f32),
            V((PIECES, Q, S, W), f32),
            V((n, code_rows(S, F), LANES), i16),
            V((n, code_rows(S, F), LANES), i16),
            V((PIECES, Q, code_rows(S, W), LANES), i16),
            V((PIECES, Q, code_rows(S, W), LANES), i16),
            V((G, code_rows(S, N), LANES), i16),
            V((G, code_rows(S, N), LANES), i16),
            V((PIECES, G, code_rows(S, W), LANES), i16),
            V((3, code_rows(S, W), LANES), i16),
            V((2, code_rows(S, W), LANES), i16),
            V((G, code_rows(S, N), LANES), i16),
            V((2 * FR, LANES), f32),
            V((2 * FR, LANES), f32),
            V((Q, 2 * FR, LANES), f32),
            V((G, 2 * FR + 8, LANES), f32),
            V((2, Q, S, LANES), f32),
            V((2, S, F), f32),
            D((NB // LOAD,)),
            D((1,)),
            D((1,)),
            D((CUTS,)),
            D((CUTS,)),
            D((1 + PIECES,)),
            D((1 + PIECES,)),
            D((2 + PIECES,)),
            D((2 + PIECES,)),
            D((2 + PIECES,)),
            D((4 + PIECES,)),
            D((3,)),
            D((3,)),
        ],
        compiler_params=pltpu.CompilerParams(
            collective_id=0, has_side_effects=True, vmem_limit_bytes=48 * 1024 * 1024
        ),
    )(pair_count, frames)
    return pl.pallas_call(
        place,
        out_shape=(
            jax.ShapeDtypeStruct((1, S, F), f32),
            jax.ShapeDtypeStruct((1, S, F), f32),
            jax.ShapeDtypeStruct((S, F), f32),
            jax.ShapeDtypeStruct((S, F), f32),
        ),
        in_specs=[vmem] * 4,
        out_specs=(vmem,) * 4,
        compiler_params=pltpu.CompilerParams(vmem_limit_bytes=4 * 1024 * 1024),
    )(*results)


def solution(mesh):
    in_specs = (P("group", "tm", None), P("group"))
    out_specs = (P("group", "tm", None), P("group", "tm", None), P("tm", None), P("tm", None))
    body = functools.partial(on_device, mesh.shape["tm"], mesh.shape["group"])
    return jax.shard_map(
        body, mesh=mesh, in_specs=in_specs, out_specs=out_specs, check_vma=False
    )
```

```python
import functools

import jax
import jax.numpy as jnp
from jax import lax
from jax.experimental import pallas as pl
from jax.experimental.pallas import tpu as pltpu
from jax.sharding import PartitionSpec as P

LAG = 2048
MESH = pl.DeviceIdType.MESH
PAD = 16
CUTS = 4
PIECES = 2
LANES = 128
LEVELS = 32700.0
STEPS = 8.0
LEAST = 1e-30
LOAD = 4


def code_rows(S, W):
    return W // LANES * S + PAD


def encode(ref, block):
    S, W = block.shape
    top = jnp.maximum(jnp.max(jnp.abs(block), axis=0, keepdims=True), LEAST)
    power = jnp.ceil(STEPS * jnp.log2(top * (1.0 / LEVELS)))
    codes = jnp.round(block * (1.0 / jnp.exp2(power * (1.0 / STEPS)))).astype(jnp.int32)
    groups = W // LANES
    for g in range(groups):
        ref[g * S:(g + 1) * S, :] = codes[:, g * LANES:(g + 1) * LANES].astype(jnp.int16)
    row = lax.broadcasted_iota(jnp.int32, (PAD, LANES), 0)
    powers = jnp.zeros((PAD, LANES), jnp.float32)
    for g in range(groups):
        part = jnp.broadcast_to(power[:, g * LANES:(g + 1) * LANES], (PAD, LANES))
        powers = jnp.where(row == g, part, powers)
    ref[groups * S:, :] = powers.astype(jnp.int32).astype(jnp.int16)


def decode(ref, S):
    groups = (ref.shape[0] - PAD) // S
    powers = ref[groups * S:, :].astype(jnp.int32).astype(jnp.float32)
    units = jnp.exp2(powers * (1.0 / STEPS))
    parts = [
        ref[g * S:(g + 1) * S, :].astype(jnp.int32).astype(jnp.float32) * units[g:g + 1]
        for g in range(groups)
    ]
    return parts[0] if groups == 1 else jnp.concatenate(parts, axis=1)


def wide(column, width):
    return jnp.concatenate([column] * (width // LANES), axis=1)


def kernel(
    T, G, count_ref, frames_ref, gi_ref, gl_ref, pi_ref, po_ref,
    x, xt, head, tail, acc, ai, al, r1i, r1l, qi, ri, ql, rl, zi, zs, zl, zh, za, zg,
    s_own, s_mate, s_chip, s_grp, cols, fix,
    ld, nears, nearr, hs, hr, s1, e1, s2, e2, sz, ez, ss, es,
):
    F = frames_ref.shape[2]
    R = frames_ref.shape[1]
    H = LAG // CUTS
    NB = R // H
    W = F // PIECES
    S = F // T
    Q = T // 2
    FR = F // LANES
    NEAR = CUTS // 2
    f32 = jnp.float32
    me = lax.axis_index("tm")
    z = lax.axis_index("group")
    c = lax.rem(me, 2)
    q = lax.div(me, 2)
    partner = me + 1 - 2 * c
    count = count_ref[0]

    def remote(src, dst, a, b, dev):
        return pltpu.make_async_remote_copy(
            src_ref=src, dst_ref=dst, send_sem=a, recv_sem=b,
            device_id=dev, device_id_type=MESH,
        )

    def load(i):
        return pltpu.make_async_copy(
            frames_ref.at[0, pl.ds(i * LOAD * H, LOAD * H)], x.at[pl.ds(i * LOAD * H, LOAD * H)], ld.at[i]
        )

    def block(j):
        return x[pl.ds(pl.multiple_of(j * H, H), H), :]

    for i in range(NB // LOAD):
        load(i).start()

    barrier = pltpu.get_barrier_semaphore()
    for k in range(1, T):
        pl.semaphore_signal(
            barrier, inc=1, device_id={"tm": lax.rem(me + k, T)}, device_id_type=MESH
        )
    for k in range(1, G):
        pl.semaphore_signal(
            barrier, inc=1, device_id={"group": lax.rem(z + k, G)}, device_id_type=MESH
        )
    with jax.named_scope("t_barrier"):
        pl.semaphore_wait(barrier, T - 1 + G - 1)

    def kept(b):
        if T != 8:
            return CUTS // 2
        turn = lax.rem(b, 2) * (1 - lax.rem(lax.div(b, 2), 2))
        return CUTS // 2 + turn * (2 * lax.div(b, 4) - 1)

    before = lax.rem(me + T - 1, T)

    near_head = remote(
        frames_ref.at[0, pl.ds(0, NEAR * H)], head.at[pl.ds(0, NEAR * H)],
        nears.at[0], nearr.at[0], {"tm": partner},
    )
    near_tail = remote(
        frames_ref.at[0, pl.ds(R - LAG + NEAR * H, (CUTS - NEAR) * H)],
        tail.at[pl.ds(NEAR * H, (CUTS - NEAR) * H)],
        nears.at[0], nearr.at[0], {"tm": partner},
    )

    def send_head(j):
        return remote(
            frames_ref.at[0, pl.ds(j * H, H)], head.at[pl.ds(j * H, H)], hs.at[j], hr.at[j],
            {"tm": me - 1},
        )

    def send_tail(j):
        return remote(
            frames_ref.at[0, pl.ds(R - LAG + j * H, H)], tail.at[pl.ds(j * H, H)], hs.at[j], hr.at[j],
            {"tm": me + 1},
        )

    def far(act, now):
        for j in range(CUTS):
            @pl.when((me > 0) & (c == 0) & (j < kept(before)) & now(kept(before) < NEAR))
            def _():
                act(send_head(j))

            @pl.when((me < T - 1) & (c == 1) & (j >= kept(me)) & now(kept(me) > NEAR))
            def _():
                act(send_tail(j))

    def sent(act):
        pl.when(c == 0)(lambda: act(near_tail))
        pl.when(c == 1)(lambda: act(near_head))

    far(lambda copy: copy.start(), jnp.logical_not)
    sent(lambda copy: copy.start())

    def put_transposed(block, base, slot):
        rows = lax.broadcasted_iota(jnp.int32, (H, LANES), 0) + base
        keep = jnp.where(rows < count, 1.0, 0.0).astype(jnp.bfloat16)
        xt[slot, 0:F, :] = (block * wide(keep, F)).T

    def put_masks(base, slot):
        frame = lax.broadcasted_iota(jnp.int32, (PAD, H), 1) + base
        kind = lax.broadcasted_iota(jnp.int32, (PAD, H), 0)
        first = jnp.where(kind == 0, 0, LAG)
        valid = (frame >= first) & (frame < first + count) & (kind < 2)
        xt[slot, F:, :] = jnp.where(valid, 1.0, 0.0).astype(jnp.bfloat16)

    def product(slot, block):
        return jnp.dot(xt[slot, 0:F, :], block, preferred_element_type=f32)

    acc[...] = jnp.zeros_like(acc)

    def inst_step(i, carry):
        @pl.when(lax.rem(2 * i, LOAD) == 0)
        def _():
            load(lax.div(2 * i, LOAD)).wait()

        for j in (2 * i, 2 * i + 1):
            put_transposed(block(j), me * R + j * H, j)
            put_masks(me * R + j * H, j)
        acc[...] += (
            jnp.dot(xt[2 * i], block(2 * i), preferred_element_type=f32)
            + jnp.dot(xt[2 * i + 1], block(2 * i + 1), preferred_element_type=f32)
        )
        return carry

    with jax.named_scope("t_inst"):
        lax.fori_loop(0, NB // 2, inst_step, 0)
    for d in range(T):
        ai[d % 2, d // 2] = acc[d * S:(d + 1) * S, :]
    for k in range(2):
        for j in range(FR):
            s_own[k * FR + j:k * FR + j + 1, :] = acc[F + k:F + k + 1, j * LANES:(j + 1) * LANES]
    p1i = remote(ai.at[1 - c], r1i, s1.at[0], e1.at[0], {"tm": partner})
    p1i.start()
    mate = remote(s_own, s_mate, ss.at[0], es.at[0], {"tm": partner})
    mate.start()

    acc[...] = jnp.zeros_like(acc)

    def lag_step(i, carry):
        j = 2 * i
        acc[0:F, :] += product(j, block(j + CUTS)) + product(j + 1, block(j + 1 + CUTS))
        return carry

    with jax.named_scope("t_lag"):
        lax.fori_loop(0, (NB - CUTS) // 2, lag_step, 0)
    far(lambda copy: copy.start(), lambda late: late)

    def clip(v, top):
        return jnp.minimum(jnp.maximum(v, 0), top)

    def vector(n):
        return jnp.broadcast_to(n, (1, LANES)).astype(f32)

    def weights(chip):
        a = chip * 2 * R
        nx = clip(count - a, 2 * R)
        ny = clip(count + LAG - a, 2 * R) - clip(LAG - a, 2 * R)
        low = jnp.where(chip > 0, kept(2 * chip - 1) * H - LAG, 0)
        high = jnp.where(chip < Q - 1, kept(2 * chip + 1) * H - LAG, 0)
        pairs = clip(count - a - low, 2 * R + high - low)
        vx, vy = vector(jnp.maximum(nx, 1)), vector(jnp.maximum(ny, 1))
        return 1.0 / vx, vector(pairs) / (vx * vy)

    lanes = lax.broadcasted_iota(jnp.int32, (S, LANES), 1)
    rows = lax.broadcasted_iota(jnp.int32, (S, LANES), 0)

    def upright(row, offset):
        picked = jnp.where(lanes == rows + offset, jnp.broadcast_to(row, (S, LANES)), 0.0)
        return jnp.broadcast_to(jnp.sum(picked, axis=1, keepdims=True), (S, LANES))

    def along(ref, kind):
        return jnp.concatenate([ref[kind * FR + j:kind * FR + j + 1, :] for j in range(FR)], axis=1)

    class Group:
        def __init__(self, a, b, like, n):
            self.pairs, self.a, self.b, self.like, self.n = [], a, b, like, n

        def send(self, src, dst, dev):
            remote(src, dst, self.a, self.b, dev).start()

        def whole(self):
            ref = self.like.at[pl.ds(0, self.n)]
            return remote(ref, ref, self.a, self.b, {"tm": partner})

        def wait_recv(self):
            self.whole().wait_recv()

        def wait_send(self):
            self.whole().wait_send()

    with jax.named_scope("t_p1i"):
        mate.wait_recv()
        s_chip[q] = s_own[...] + s_mate[...]
        chips = Group(ss.at[1], es.at[1], s_chip, Q - 1)
        for k in range(1, Q):
            chips.send(s_chip.at[q], s_chip.at[q], {"tm": 2 * lax.rem(q + k, Q) + c})
        wx, wl = weights(q)
        mine = s_chip.at[q]
        for k in range(Q):
            at = 2 * k * S
            col = upright(mine[at // LANES:at // LANES + 1, :], at % LANES + c * S)
            cols[0, k] = col * wx
            cols[1, k] = col * wl
        p1i.wait_recv()
        sx = along(mine, 0)
        for k in range(Q):
            ai[c, k] = ai[c, k] + r1i[k] - wide(cols[0, k], F) * sx

    square = Q == 4
    with jax.named_scope("t_inst_send"):
        if square:
            side, level = lax.rem(q, 2), lax.div(q, 2)
            across = q + 1 - 2 * side
            for k in range(2):
                encode(qi.at[k], ai[c, 2 - 2 * level + k])
            over = remote(
                qi.at[pl.ds(0, 2)], ri.at[pl.ds(0, 2)], s2.at[0], e2.at[0],
                {"tm": 2 * lax.rem(q + 2, Q) + c},
            )
            over.start()
            p2i = remote(qi.at[2], ri.at[2], s2.at[1], e2.at[1], {"tm": 2 * across + c})
        else:
            p2i = Group(s2.at[1], e2.at[1], ri, Q - 1)
            for k in range(1, Q):
                q2 = lax.rem(q + k, Q)
                encode(qi.at[k - 1], ai[c, q2])
                p2i.send(qi.at[k - 1], ri.at[k - 1], {"tm": 2 * q2 + c})

    def take_head(j):
        acc[0:F, :] += product(NB - CUTS + j, head[pl.ds(pl.multiple_of(j * H, H), H), :])

    def take_tail(j):
        put_transposed(tail[pl.ds(pl.multiple_of(j * H, H), H), :], me * R - LAG + j * H, j)
        acc[0:F, :] += product(j, block(j))

    def near_heads():
        near_head.wait_recv()

        def step(j, carry):
            take_head(j)
            return carry

        lax.fori_loop(0, NEAR, step, 0)

    def near_tails():
        near_tail.wait_recv()

        def step(j, carry):
            take_tail(j)
            return carry

        lax.fori_loop(NEAR, CUTS, step, 0)

    def relay_instant():
        over.wait_recv()
        for k in range(2):
            ai[c, 2 * level + k] += decode(ri.at[k], S)
        encode(qi.at[2], ai[c, across])
        p2i.start()

    def far_heads():
        def step(j, carry):
            send_head(j).wait_recv()
            take_head(j)
            return carry

        lax.fori_loop(0, kept(me) - 1, step, 0)
        if square:
            pl.when(kept(me) > 1)(relay_instant)
        step(kept(me) - 1, 0)

    def far_tails():
        def step(j, carry):
            send_tail(j).wait_recv()
            take_tail(j)
            return carry

        lax.fori_loop(kept(before), CUTS - 1, step, 0)
        if square:
            pl.when(kept(before) < CUTS - 1)(relay_instant)
        step(CUTS - 1, 0)

    with jax.named_scope("t_halo_near"):
        pl.when(c == 0)(near_heads)
        pl.when(c == 1)(near_tails)
    with jax.named_scope("t_halo_far"):
        has_heads = (me < T - 1) & (c == 1)
        has_tails = (me > 0) & (c == 0)
        pl.when(has_heads)(far_heads)
        pl.when(has_tails)(far_tails)

    with jax.named_scope("t_lag_out"):
        p1l = []
        for h in range(PIECES):
            for d in range(T):
                al[h, d % 2, d // 2] = acc[d * S:(d + 1) * S, h * W:(h + 1) * W]
            p1l.append(
                remote(al.at[h, 1 - c], r1l.at[h], s1.at[1 + h], e1.at[1 + h], {"tm": partner})
            )
            p1l[h].start()

    with jax.named_scope("t_inst_x"):
        if square:
            early = (has_heads & (kept(me) > 1)) | (has_tails & (kept(before) < CUTS - 1))
            pl.when(jnp.logical_not(early))(relay_instant)

    with jax.named_scope("t_p1l"):
        p2l = [Group(s2.at[2 + h], e2.at[2 + h], rl.at[h], Q - 1) for h in range(PIECES)]

        def spread(h, chip):
            @pl.when(chip != q)
            def _():
                sy = along(mine, 1)[:, h * W:(h + 1) * W]
                encode(
                    ql.at[h, chip], al[h, c, chip] + r1l[h, chip] - wide(cols[1, chip], W) * sy
                )
                p2l[h].send(ql.at[h, chip], rl.at[h, q], {"tm": 2 * chip + c})

        for h in range(PIECES):
            p1l[h].wait_recv()
            spread(h, 0)
        for h in range(PIECES):
            for chip in range(1, Q):
                spread(h, chip)
            sy = along(mine, 1)[:, h * W:(h + 1) * W]
            al[h, c, q] = al[h, c, q] + r1l[h, q] - wide(cols[1, q], W) * sy

    with jax.named_scope("t_sums"):
        chips.wait_recv()

        at = lax.div(me * S, LANES)
        off = lax.rem(me * S, LANES)

        def outer(ref, kind, scale):
            return wide(upright(ref[pl.ds(at, 1), :], off) * scale, F) * along(ref, kind)

        total = s_chip[0]
        for k in range(1, Q):
            total = total + s_chip[k]
        s_grp[z, 0:2 * FR, :] = total
        s_grp[z, 2 * FR:, :] = jnp.broadcast_to(vector(count), (8, LANES))
        groups = Group(ss.at[2], es.at[2], s_grp, G - 1)
        for k in range(1, G):
            groups.send(s_grp.at[z], s_grp.at[z], {"group": lax.rem(z + k, G)})
        number = vector(count)
        for kind in range(2):
            term = -outer(s_grp.at[z], kind, 1.0 / number)
            for k in range(Q):
                term = term + outer(s_chip.at[k], kind, weights(k)[kind])
            fix[kind] = term
        count_f = wide(number, F)

    def to_groups(group, buf):
        for i in range(G):
            w = jnp.where(c == 0, i, G - 1 - i)

            @pl.when(w != z)
            def _():
                group.send(buf.at[z], buf.at[z], {"group": w})

    shares = G if F % (G * LANES) == 0 else 1
    N = F // shares
    with jax.named_scope("t_zi"):
        p2i.wait_recv()
        total = ai[c, q] + fix[0]
        for k in ((2,) if square else range(Q - 1)):
            total = total + decode(ri.at[k], S)
        gi_ref[...] = total / count_f
        part_sums = Group(sz.at[0], ez.at[0], zs, G - 1)
        full_sums = Group(sz.at[1], ez.at[1], zi, G - 1)
        if shares == G:
            for w in range(G):
                cut = total[:, w * N:(w + 1) * N]

                @pl.when(w != z)
                def _():
                    encode(zi.at[w], cut)
                    part_sums.send(zi.at[w], zs.at[z], {"group": w})

                @pl.when(w == z)
                def _():
                    ai[c, q, :, 0:N] = cut
        else:
            encode(zi.at[z], total)
            to_groups(full_sums, zi)

    hub = G == 4
    zl_groups = []
    if hub:
        inner = (z == 1) | (z == 2)
        neighbour = jnp.where(z < 2, 1, 2)
        direct = Group(sz.at[2], ez.at[6], za, G - 1)

        def inward(slot):
            return remote(za.at[slot], za.at[slot], sz.at[2], ez.at[2], {"group": neighbour})

        def onward(k, w):
            return remote(zh.at[k], zh.at[k], sz.at[2], ez.at[4 + k], {"group": w})

    def lag_session(h):
        with jax.named_scope("t_p2l"):
            p2l[h].wait_recv()
            part = slice(h * W, (h + 1) * W)
            total = al[h, c, q] + fix[1, :, part]
            for k in range(1, Q):
                total = total + decode(rl.at[h, lax.rem(q + k, Q)], S)
            gl_ref[:, part] = total / count_f[:, part]
            if hub and h == 0:
                encode(za.at[z], total)

                @pl.when(jnp.logical_not(inner))
                def _():
                    inward(z).start()

                @pl.when(z > 0)
                def _():
                    direct.send(za.at[z], za.at[z], {"group": 0})

            else:
                encode(zl.at[h, z], total)
                zl_groups.append(Group(sz.at[2 + h], ez.at[2 + h], zl.at[h], G - 1))
                to_groups(zl_groups[-1], zl.at[h])

    lag_session(0)
    if shares == G:
        with jax.named_scope("t_zi_share"):
            part_sums.wait_recv()
            total = ai[c, q, :, 0:N]
            for k in range(1, G):
                total = total + decode(zs.at[lax.rem(z + k, G)], S)
            encode(zg.at[z], total)
            full_sums = Group(sz.at[1], ez.at[1], zg, G - 1)
            to_groups(full_sums, zg)
    for h in range(1, PIECES):
        lag_session(h)
    if hub:
        with jax.named_scope("t_hub"):
            @pl.when(inner)
            def _():
                inward(3 * (z - 1)).wait_recv()

            pl.when(z == 0)(direct.wait_recv)
            for k in range(2):
                @pl.when((z == 0) | (z == 1 + k))
                def _():
                    encode(zh.at[k], decode(za.at[2 * k], S) + decode(za.at[2 * k + 1], S))

                @pl.when(z == 1 + k)
                def _():
                    for w in (2 - k, 3):
                        onward(k, w).start()

    with jax.named_scope("t_pool"):
        groups.wait_recv()
        everyone = s_grp[0]
        for k in range(1, G):
            everyone = everyone + s_grp[k]
        s_mate[...] = everyone[0:2 * FR]
        all_n = everyone[2 * FR:2 * FR + 1]
        for kind in range(2):
            term = -outer(s_mate, kind, 1.0 / all_n)
            for k in range(G):
                term = term + outer(s_grp.at[k], kind, 1.0 / s_grp[k, 2 * FR:2 * FR + 1, :])
            fix[kind] = term
        whole_f = wide(all_n, F)

    def pooled(h):
        part = slice(h * W, (h + 1) * W)
        total = fix[1, :, part]
        if hub and h == 0:
            for k in range(2):
                total = total + decode(zh.at[k], S)
        else:
            for k in range(G):
                total = total + decode(zl.at[h, k], S)
        po_ref[:, part] = total / whole_f[:, part]

    for h in range(1 if hub else 0, PIECES):
        with jax.named_scope("t_zl_in"):
            zl_groups[h - PIECES].wait_recv()
            pooled(h)
    if hub:
        with jax.named_scope("t_hub_in"):
            for k in range(2):
                pl.when((z == 3) | (z == 2 - k))(onward(k, 3).wait_recv)
            pooled(0)

    with jax.named_scope("t_zi_in"):
        full_sums.wait_recv()
        if shares == G:
            for w in range(G):
                part = slice(w * N, (w + 1) * N)
                pi_ref[:, part] = (fix[0, :, part] + decode(zg.at[w], S)) / whole_f[:, part]
        else:
            total = fix[0]
            for k in range(G):
                total = total + decode(zi.at[k], S)
            pi_ref[...] = total / whole_f

    with jax.named_scope("t_end"):
        sent(lambda copy: copy.wait_send())
        far(lambda copy: copy.wait_send(), lambda late: late)
        far(lambda copy: copy.wait_send(), jnp.logical_not)
        if square:
            over.wait_send()
        if shares == G:
            part_sums.wait_send()
        if hub:
            for n, which in ((1, z == 0), (2, z == 3), (3, inner)):
                pl.when(which)(Group(sz.at[2], ez.at[6], za, n).wait_send)
        for copy in [p1i, mate, chips, groups, *p1l, p2i, *p2l, full_sums, *zl_groups]:
            copy.wait_send()


def place(gi, gl, pi, po, gi_out, gl_out, pi_out, po_out):
    gi_out[0] = gi[...]
    gl_out[0] = gl[...]
    pi_out[...] = pi[...]
    po_out[...] = po[...]


def on_device(T, G, frames, pair_count):
    _, R, F = frames.shape
    S, Q, H, W = F // T, T // 2, LAG // CUTS, F // PIECES
    NB = R // H
    FR = F // LANES
    f32, bf16, i16 = jnp.float32, jnp.bfloat16, jnp.int16
    V, D = pltpu.VMEM, pltpu.SemaphoreType.DMA
    vmem = pl.BlockSpec(memory_space=pltpu.VMEM)
    n = max(Q - 1, 3)
    N = F // G if F % (G * LANES) == 0 else F
    results = pl.pallas_call(
        functools.partial(kernel, T, G),
        out_shape=(jax.ShapeDtypeStruct((S, F), f32),) * 4,
        in_specs=[pl.BlockSpec(memory_space=pltpu.SMEM), pl.BlockSpec(memory_space=pl.ANY)],
        out_specs=(vmem,) * 4,
        scratch_shapes=[
            V((R, F), bf16),
            V((NB, F + PAD, H), bf16),
            V((LAG, F), bf16),
            V((LAG, F), bf16),
            V((F + PAD, F), f32),
            V((2, Q, S, F), f32),
            V((PIECES, 2, Q, S, W), f32),
            V((Q, S, F), f32),
            V((PIECES, Q, S, W), f32),
            V((n, code_rows(S, F), LANES), i16),
            V((n, code_rows(S, F), LANES), i16),
            V((PIECES, Q, code_rows(S, W), LANES), i16),
            V((PIECES, Q, code_rows(S, W), LANES), i16),
            V((G, code_rows(S, N), LANES), i16),
            V((G, code_rows(S, N), LANES), i16),
            V((PIECES, G, code_rows(S, W), LANES), i16),
            V((2, code_rows(S, W), LANES), i16),
            V((4, code_rows(S, W), LANES), i16),
            V((G, code_rows(S, N), LANES), i16),
            V((2 * FR, LANES), f32),
            V((2 * FR, LANES), f32),
            V((Q, 2 * FR, LANES), f32),
            V((G, 2 * FR + 8, LANES), f32),
            V((2, Q, S, LANES), f32),
            V((2, S, F), f32),
            D((NB // LOAD,)),
            D((1,)),
            D((1,)),
            D((CUTS,)),
            D((CUTS,)),
            D((1 + PIECES,)),
            D((1 + PIECES,)),
            D((2 + PIECES,)),
            D((2 + PIECES,)),
            D((2 + PIECES,)),
            D((5 + PIECES,)),
            D((3,)),
            D((3,)),
        ],
        compiler_params=pltpu.CompilerParams(
            collective_id=0, has_side_effects=True, vmem_limit_bytes=48 * 1024 * 1024
        ),
    )(pair_count, frames)
    return pl.pallas_call(
        place,
        out_shape=(
            jax.ShapeDtypeStruct((1, S, F), f32),
            jax.ShapeDtypeStruct((1, S, F), f32),
            jax.ShapeDtypeStruct((S, F), f32),
            jax.ShapeDtypeStruct((S, F), f32),
        ),
        in_specs=[vmem] * 4,
        out_specs=(vmem,) * 4,
        compiler_params=pltpu.CompilerParams(vmem_limit_bytes=4 * 1024 * 1024),
    )(*results)


def solution(mesh):
    in_specs = (P("group", "tm", None), P("group"))
    out_specs = (P("group", "tm", None), P("group", "tm", None), P("tm", None), P("tm", None))
    body = functools.partial(on_device, mesh.shape["tm"], mesh.shape["group"])
    return jax.shard_map(
        body, mesh=mesh, in_specs=in_specs, out_specs=out_specs, check_vma=False
    )
```

```python
import functools

import jax
import jax.numpy as jnp
from jax import lax
from jax.experimental import pallas as pl
from jax.experimental.pallas import tpu as pltpu
from jax.sharding import PartitionSpec as P

LAG = 2048
MESH = pl.DeviceIdType.MESH
PAD = 16
CUTS = 4
PIECES = 2
LANES = 128
LEVELS = 32700.0
STEPS = 8.0
LEAST = 1e-30
LOAD = 8


def code_rows(S, W):
    return W // LANES * S + PAD


def encode(ref, block):
    S, W = block.shape
    top = jnp.maximum(jnp.max(jnp.abs(block), axis=0, keepdims=True), LEAST)
    power = jnp.ceil(STEPS * jnp.log2(top * (1.0 / LEVELS)))
    codes = jnp.round(block * (1.0 / jnp.exp2(power * (1.0 / STEPS)))).astype(jnp.int32)
    groups = W // LANES
    for g in range(groups):
        ref[g * S:(g + 1) * S, :] = codes[:, g * LANES:(g + 1) * LANES].astype(jnp.int16)
    row = lax.broadcasted_iota(jnp.int32, (PAD, LANES), 0)
    powers = jnp.zeros((PAD, LANES), jnp.float32)
    for g in range(groups):
        part = jnp.broadcast_to(power[:, g * LANES:(g + 1) * LANES], (PAD, LANES))
        powers = jnp.where(row == g, part, powers)
    ref[groups * S:, :] = powers.astype(jnp.int32).astype(jnp.int16)


def decode(ref, S):
    groups = (ref.shape[0] - PAD) // S
    powers = ref[groups * S:, :].astype(jnp.int32).astype(jnp.float32)
    units = jnp.exp2(powers * (1.0 / STEPS))
    parts = [
        ref[g * S:(g + 1) * S, :].astype(jnp.int32).astype(jnp.float32) * units[g:g + 1]
        for g in range(groups)
    ]
    return parts[0] if groups == 1 else jnp.concatenate(parts, axis=1)


def wide(column, width):
    return jnp.concatenate([column] * (width // LANES), axis=1)


def kernel(
    T, G, count_ref, frames_ref, gi_ref, gl_ref, pi_ref, po_ref,
    x, xt, head, tail, acc, ai, al, r1i, r1l, qi, ri, ql, rl, zi, zs, zl, zh, za, zg,
    s_own, s_mate, s_chip, s_grp, cols, fix,
    ld, nears, nearr, hs, hr, s1, e1, s2, e2, sz, ez, ss, es,
):
    F = frames_ref.shape[2]
    R = frames_ref.shape[1]
    H = LAG // CUTS
    NB = R // H
    W = F // PIECES
    S = F // T
    Q = T // 2
    FR = F // LANES
    NEAR = CUTS // 2
    f32 = jnp.float32
    me = lax.axis_index("tm")
    z = lax.axis_index("group")
    c = lax.rem(me, 2)
    q = lax.div(me, 2)
    partner = me + 1 - 2 * c
    count = count_ref[0]

    def remote(src, dst, a, b, dev):
        return pltpu.make_async_remote_copy(
            src_ref=src, dst_ref=dst, send_sem=a, recv_sem=b,
            device_id=dev, device_id_type=MESH,
        )

    def load(i):
        return pltpu.make_async_copy(
            frames_ref.at[0, pl.ds(i * LOAD * H, LOAD * H)], x.at[pl.ds(i * LOAD * H, LOAD * H)], ld.at[i]
        )

    def block(j):
        return x[pl.ds(pl.multiple_of(j * H, H), H), :]

    for i in range(NB // LOAD):
        load(i).start()

    barrier = pltpu.get_barrier_semaphore()
    for k in range(1, T):
        pl.semaphore_signal(
            barrier, inc=1, device_id={"tm": lax.rem(me + k, T)}, device_id_type=MESH
        )
    for k in range(1, G):
        pl.semaphore_signal(
            barrier, inc=1, device_id={"group": lax.rem(z + k, G)}, device_id_type=MESH
        )
    with jax.named_scope("t_barrier"):
        pl.semaphore_wait(barrier, T - 1 + G - 1)

    def kept(b):
        if T != 8:
            return CUTS // 2
        turn = lax.rem(b, 2) * (1 - lax.rem(lax.div(b, 2), 2))
        return CUTS // 2 + turn * (2 * lax.div(b, 4) - 1)

    before = lax.rem(me + T - 1, T)

    near_head = remote(
        frames_ref.at[0, pl.ds(0, NEAR * H)], head.at[pl.ds(0, NEAR * H)],
        nears.at[0], nearr.at[0], {"tm": partner},
    )
    near_tail = remote(
        frames_ref.at[0, pl.ds(R - LAG + NEAR * H, (CUTS - NEAR) * H)],
        tail.at[pl.ds(NEAR * H, (CUTS - NEAR) * H)],
        nears.at[0], nearr.at[0], {"tm": partner},
    )

    def send_head(j):
        return remote(
            frames_ref.at[0, pl.ds(j * H, H)], head.at[pl.ds(j * H, H)], hs.at[j], hr.at[j],
            {"tm": me - 1},
        )

    def send_tail(j):
        return remote(
            frames_ref.at[0, pl.ds(R - LAG + j * H, H)], tail.at[pl.ds(j * H, H)], hs.at[j - 1], hr.at[j - 1],
            {"tm": me + 1},
        )

    def far(act, now):
        for j in range(CUTS - 1):
            @pl.when((me > 0) & (c == 0) & (j < kept(before)) & now(kept(before) < NEAR))
            def _():
                act(send_head(j))

        for j in range(1, CUTS):
            @pl.when((me < T - 1) & (c == 1) & (j >= kept(me)) & now(kept(me) > NEAR))
            def _():
                act(send_tail(j))

    def sent(act):
        pl.when(c == 0)(lambda: act(near_tail))
        pl.when(c == 1)(lambda: act(near_head))

    far(lambda copy: copy.start(), jnp.logical_not)
    sent(lambda copy: copy.start())

    def put_transposed(block, base, slot):
        rows = lax.broadcasted_iota(jnp.int32, (H, LANES), 0) + base
        keep = jnp.where(rows < count, 1.0, 0.0).astype(jnp.bfloat16)
        xt[slot, 0:F, :] = (block * wide(keep, F)).T

    def put_masks(base, slot):
        frame = lax.broadcasted_iota(jnp.int32, (PAD, H), 1) + base
        kind = lax.broadcasted_iota(jnp.int32, (PAD, H), 0)
        first = jnp.where(kind == 0, 0, LAG)
        valid = (frame >= first) & (frame < first + count) & (kind < 2)
        xt[slot, F:, :] = jnp.where(valid, 1.0, 0.0).astype(jnp.bfloat16)

    def product(slot, block):
        return jnp.dot(xt[slot, 0:F, :], block, preferred_element_type=f32)

    acc[...] = jnp.zeros_like(acc)

    def inst_step(i, carry):
        @pl.when(lax.rem(2 * i, LOAD) == 0)
        def _():
            load(lax.div(2 * i, LOAD)).wait()

        for j in (2 * i, 2 * i + 1):
            put_transposed(block(j), me * R + j * H, j)
            put_masks(me * R + j * H, j)
        acc[...] += (
            jnp.dot(xt[2 * i], block(2 * i), preferred_element_type=f32)
            + jnp.dot(xt[2 * i + 1], block(2 * i + 1), preferred_element_type=f32)
        )
        return carry

    with jax.named_scope("t_inst"):
        lax.fori_loop(0, NB // 2, inst_step, 0)
    for d in range(T):
        ai[d % 2, d // 2] = acc[d * S:(d + 1) * S, :]
    for k in range(2):
        for j in range(FR):
            s_own[k * FR + j:k * FR + j + 1, :] = acc[F + k:F + k + 1, j * LANES:(j + 1) * LANES]
    p1i = remote(ai.at[1 - c], r1i, s1.at[0], e1.at[0], {"tm": partner})
    p1i.start()
    mate = remote(s_own, s_mate, ss.at[0], es.at[0], {"tm": partner})
    mate.start()

    acc[...] = jnp.zeros_like(acc)

    def lag_step(i, carry):
        j = 2 * i
        acc[0:F, :] += product(j, block(j + CUTS)) + product(j + 1, block(j + 1 + CUTS))
        return carry

    with jax.named_scope("t_lag"):
        lax.fori_loop(0, (NB - CUTS) // 2, lag_step, 0)
    far(lambda copy: copy.start(), lambda late: late)

    def clip(v, top):
        return jnp.minimum(jnp.maximum(v, 0), top)

    def vector(n):
        return jnp.broadcast_to(n, (1, LANES)).astype(f32)

    def weights(chip):
        a = chip * 2 * R
        nx = clip(count - a, 2 * R)
        ny = clip(count + LAG - a, 2 * R) - clip(LAG - a, 2 * R)
        low = jnp.where(chip > 0, kept(2 * chip - 1) * H - LAG, 0)
        high = jnp.where(chip < Q - 1, kept(2 * chip + 1) * H - LAG, 0)
        pairs = clip(count - a - low, 2 * R + high - low)
        vx, vy = vector(jnp.maximum(nx, 1)), vector(jnp.maximum(ny, 1))
        return 1.0 / vx, vector(pairs) / (vx * vy)

    lanes = lax.broadcasted_iota(jnp.int32, (S, LANES), 1)
    rows = lax.broadcasted_iota(jnp.int32, (S, LANES), 0)

    def upright(row, offset):
        picked = jnp.where(lanes == rows + offset, jnp.broadcast_to(row, (S, LANES)), 0.0)
        return jnp.broadcast_to(jnp.sum(picked, axis=1, keepdims=True), (S, LANES))

    def along(ref, kind):
        return jnp.concatenate([ref[kind * FR + j:kind * FR + j + 1, :] for j in range(FR)], axis=1)

    class Group:
        def __init__(self, a, b, like, n):
            self.pairs, self.a, self.b, self.like, self.n = [], a, b, like, n

        def send(self, src, dst, dev):
            remote(src, dst, self.a, self.b, dev).start()

        def whole(self):
            ref = self.like.at[pl.ds(0, self.n)]
            return remote(ref, ref, self.a, self.b, {"tm": partner})

        def wait_recv(self):
            self.whole().wait_recv()

        def wait_send(self):
            self.whole().wait_send()

    with jax.named_scope("t_p1i"):
        mate.wait_recv()
        s_chip[q] = s_own[...] + s_mate[...]
        chips = Group(ss.at[1], es.at[1], s_chip, Q - 1)
        for k in range(1, Q):
            chips.send(s_chip.at[q], s_chip.at[q], {"tm": 2 * lax.rem(q + k, Q) + c})
        wx, wl = weights(q)
        mine = s_chip.at[q]
        for k in range(Q):
            at = 2 * k * S
            col = upright(mine[at // LANES:at // LANES + 1, :], at % LANES + c * S)
            cols[0, k] = col * wx
            cols[1, k] = col * wl
        p1i.wait_recv()
        sx = along(mine, 0)
        for k in range(Q):
            ai[c, k] = ai[c, k] + r1i[k] - wide(cols[0, k], F) * sx

    square = Q == 4
    with jax.named_scope("t_inst_send"):
        if square:
            side, level = lax.rem(q, 2), lax.div(q, 2)
            across = q + 1 - 2 * side
            for k in range(2):
                encode(qi.at[k], ai[c, 2 - 2 * level + k])
            over = remote(
                qi.at[pl.ds(0, 2)], ri.at[pl.ds(0, 2)], s2.at[0], e2.at[0],
                {"tm": 2 * lax.rem(q + 2, Q) + c},
            )
            over.start()
            p2i = remote(qi.at[2], ri.at[2], s2.at[1], e2.at[1], {"tm": 2 * across + c})
        else:
            p2i = Group(s2.at[1], e2.at[1], ri, Q - 1)
            for k in range(1, Q):
                q2 = lax.rem(q + k, Q)
                encode(qi.at[k - 1], ai[c, q2])
                p2i.send(qi.at[k - 1], ri.at[k - 1], {"tm": 2 * q2 + c})

    def take_head(j):
        acc[0:F, :] += product(NB - CUTS + j, head[pl.ds(pl.multiple_of(j * H, H), H), :])

    def take_tail(j):
        put_transposed(tail[pl.ds(pl.multiple_of(j * H, H), H), :], me * R - LAG + j * H, j)
        acc[0:F, :] += product(j, block(j))

    def near_heads():
        near_head.wait_recv()

        def step(j, carry):
            take_head(j)
            return carry

        lax.fori_loop(0, NEAR, step, 0)

    def near_tails():
        near_tail.wait_recv()

        def step(j, carry):
            take_tail(j)
            return carry

        lax.fori_loop(NEAR, CUTS, step, 0)

    def relay_instant():
        over.wait_recv()
        for k in range(2):
            ai[c, 2 * level + k] += decode(ri.at[k], S)
        encode(qi.at[2], ai[c, across])
        p2i.start()

    def far_heads():
        def step(j, carry):
            send_head(j).wait_recv()
            take_head(j)
            return carry

        lax.fori_loop(0, kept(me) - 1, step, 0)
        if square:
            pl.when(kept(me) > 1)(relay_instant)
        step(kept(me) - 1, 0)

    def far_tails():
        def step(j, carry):
            send_tail(j).wait_recv()
            take_tail(j)
            return carry

        lax.fori_loop(kept(before), CUTS - 1, step, 0)
        if square:
            pl.when(kept(before) < CUTS - 1)(relay_instant)
        step(CUTS - 1, 0)

    with jax.named_scope("t_halo_near"):
        pl.when(c == 0)(near_heads)
        pl.when(c == 1)(near_tails)
    with jax.named_scope("t_halo_far"):
        has_heads = (me < T - 1) & (c == 1)
        has_tails = (me > 0) & (c == 0)
        pl.when(has_heads)(far_heads)
        pl.when(has_tails)(far_tails)

    with jax.named_scope("t_lag_out"):
        p1l = []
        for h in range(PIECES):
            for d in range(T):
                al[h, d % 2, d // 2] = acc[d * S:(d + 1) * S, h * W:(h + 1) * W]
            p1l.append(
                remote(al.at[h, 1 - c], r1l.at[h], s1.at[0], e1.at[1 + h], {"tm": partner})
            )
            p1l[h].start()

    with jax.named_scope("t_inst_x"):
        if square:
            early = (has_heads & (kept(me) > 1)) | (has_tails & (kept(before) < CUTS - 1))
            pl.when(jnp.logical_not(early))(relay_instant)

    with jax.named_scope("t_p1l"):
        p2l = [Group(s2.at[2 + h], e2.at[2 + h], rl.at[h], Q - 1) for h in range(PIECES)]

        def spread(h, chip):
            @pl.when(chip != q)
            def _():
                sy = along(mine, 1)[:, h * W:(h + 1) * W]
                encode(
                    ql.at[h, chip], al[h, c, chip] + r1l[h, chip] - wide(cols[1, chip], W) * sy
                )
                p2l[h].send(ql.at[h, chip], rl.at[h, q], {"tm": 2 * chip + c})

        for h in range(PIECES):
            p1l[h].wait_recv()
            for chip in range(Q):
                spread(h, chip)
            sy = along(mine, 1)[:, h * W:(h + 1) * W]
            al[h, c, q] = al[h, c, q] + r1l[h, q] - wide(cols[1, q], W) * sy

    with jax.named_scope("t_sums"):
        chips.wait_recv()

        at = lax.div(me * S, LANES)
        off = lax.rem(me * S, LANES)

        def outer(ref, kind, scale):
            return wide(upright(ref[pl.ds(at, 1), :], off) * scale, F) * along(ref, kind)

        total = s_chip[0]
        for k in range(1, Q):
            total = total + s_chip[k]
        s_grp[z, 0:2 * FR, :] = total
        s_grp[z, 2 * FR:, :] = jnp.broadcast_to(vector(count), (8, LANES))
        groups = Group(ss.at[2], es.at[2], s_grp, G - 1)
        for k in range(1, G):
            groups.send(s_grp.at[z], s_grp.at[z], {"group": lax.rem(z + k, G)})
        number = vector(count)
        for kind in range(2):
            term = -outer(s_grp.at[z], kind, 1.0 / number)
            for k in range(Q):
                term = term + outer(s_chip.at[k], kind, weights(k)[kind])
            fix[kind] = term
        count_f = wide(number, F)

    def to_groups(group, buf):
        for i in range(G):
            w = jnp.where(c == 0, i, G - 1 - i)

            @pl.when(w != z)
            def _():
                group.send(buf.at[z], buf.at[z], {"group": w})

    shares = G if F % (G * LANES) == 0 else 1
    N = F // shares
    with jax.named_scope("t_zi"):
        p2i.wait_recv()
        total = ai[c, q] + fix[0]
        for k in ((2,) if square else range(Q - 1)):
            total = total + decode(ri.at[k], S)
        gi_ref[...] = total / count_f
        part_sums = Group(sz.at[0], ez.at[0], zs, G - 1)
        full_sums = Group(sz.at[1], ez.at[1], zi, G - 1)
        if shares == G:
            for w in range(G):
                cut = total[:, w * N:(w + 1) * N]

                @pl.when(w != z)
                def _():
                    encode(zi.at[w], cut)
                    part_sums.send(zi.at[w], zs.at[z], {"group": w})

                @pl.when(w == z)
                def _():
                    ai[c, q, :, 0:N] = cut
        else:
            encode(zi.at[z], total)
            to_groups(full_sums, zi)

    hub = G == 4
    zl_groups = []
    if hub:
        inner = (z == 1) | (z == 2)
        neighbour = jnp.where(z < 2, 1, 2)
        direct = Group(sz.at[2], ez.at[6], za, G - 1)

        def inward(slot):
            return remote(za.at[slot], za.at[slot], sz.at[2], ez.at[2], {"group": neighbour})

        def onward(k, w):
            return remote(zh.at[k], zh.at[k], sz.at[2], ez.at[4 + k], {"group": w})

    def lag_session(h):
        with jax.named_scope("t_p2l"):
            p2l[h].wait_recv()
            part = slice(h * W, (h + 1) * W)
            total = al[h, c, q] + fix[1, :, part]
            for k in range(1, Q):
                total = total + decode(rl.at[h, lax.rem(q + k, Q)], S)
            gl_ref[:, part] = total / count_f[:, part]
            if hub and h == 0:
                encode(za.at[z], total)

                @pl.when(jnp.logical_not(inner))
                def _():
                    inward(z).start()

                @pl.when(z > 0)
                def _():
                    direct.send(za.at[z], za.at[z], {"group": 0})

            else:
                encode(zl.at[h, z], total)
                zl_groups.append(Group(sz.at[2 + h], ez.at[2 + h], zl.at[h], G - 1))
                to_groups(zl_groups[-1], zl.at[h])

    lag_session(0)
    if shares == G:
        with jax.named_scope("t_zi_share"):
            part_sums.wait_recv()
            total = ai[c, q, :, 0:N]
            for k in range(1, G):
                total = total + decode(zs.at[lax.rem(z + k, G)], S)
            encode(zg.at[z], total)
            full_sums = Group(sz.at[1], ez.at[1], zg, G - 1)
            to_groups(full_sums, zg)
    for h in range(1, PIECES):
        lag_session(h)
    if hub:
        with jax.named_scope("t_hub"):
            @pl.when(inner)
            def _():
                inward(3 * (z - 1)).wait_recv()

            pl.when(z == 0)(direct.wait_recv)
            for k in range(2):
                @pl.when((z == 0) | (z == 1 + k))
                def _():
                    encode(zh.at[k], decode(za.at[2 * k], S) + decode(za.at[2 * k + 1], S))

                @pl.when(z == 1 + k)
                def _():
                    for w in (2 - k, 3):
                        onward(k, w).start()

    with jax.named_scope("t_pool"):
        groups.wait_recv()
        everyone = s_grp[0]
        for k in range(1, G):
            everyone = everyone + s_grp[k]
        s_mate[...] = everyone[0:2 * FR]
        all_n = everyone[2 * FR:2 * FR + 1]
        for kind in range(2):
            term = -outer(s_mate, kind, 1.0 / all_n)
            for k in range(G):
                term = term + outer(s_grp.at[k], kind, 1.0 / s_grp[k, 2 * FR:2 * FR + 1, :])
            fix[kind] = term
        whole_f = wide(all_n, F)

    def pooled(h):
        part = slice(h * W, (h + 1) * W)
        total = fix[1, :, part]
        if hub and h == 0:
            for k in range(2):
                total = total + decode(zh.at[k], S)
        else:
            for k in range(G):
                total = total + decode(zl.at[h, k], S)
        po_ref[:, part] = total / whole_f[:, part]

    for h in range(1 if hub else 0, PIECES):
        with jax.named_scope("t_zl_in"):
            zl_groups[h - PIECES].wait_recv()
            pooled(h)
    if hub:
        with jax.named_scope("t_hub_in"):
            for k in range(2):
                pl.when((z == 3) | (z == 2 - k))(onward(k, 3).wait_recv)
            pooled(0)

    with jax.named_scope("t_zi_in"):
        full_sums.wait_recv()
        if shares == G:
            for w in range(G):
                part = slice(w * N, (w + 1) * N)
                pi_ref[:, part] = (fix[0, :, part] + decode(zg.at[w], S)) / whole_f[:, part]
        else:
            total = fix[0]
            for k in range(G):
                total = total + decode(zi.at[k], S)
            pi_ref[...] = total / whole_f

    with jax.named_scope("t_end"):
        sent(lambda copy: copy.wait_send())
        far(lambda copy: copy.wait_send(), lambda late: late)
        far(lambda copy: copy.wait_send(), jnp.logical_not)
        if square:
            over.wait_send()
        if shares == G:
            part_sums.wait_send()
        if hub:
            for n, which in ((1, z == 0), (2, z == 3), (3, inner)):
                pl.when(which)(Group(sz.at[2], ez.at[6], za, n).wait_send)
        remote(ai, ai, s1.at[0], e1.at[0], {"tm": partner}).wait_send()
        for copy in [mate, chips, groups, p2i, *p2l, full_sums, *zl_groups]:
            copy.wait_send()


def place(gi, gl, pi, po, gi_out, gl_out, pi_out, po_out):
    gi_out[0] = gi[...]
    gl_out[0] = gl[...]
    pi_out[...] = pi[...]
    po_out[...] = po[...]


def on_device(T, G, frames, pair_count):
    _, R, F = frames.shape
    S, Q, H, W = F // T, T // 2, LAG // CUTS, F // PIECES
    NB = R // H
    FR = F // LANES
    f32, bf16, i16 = jnp.float32, jnp.bfloat16, jnp.int16
    V, D = pltpu.VMEM, pltpu.SemaphoreType.DMA
    vmem = pl.BlockSpec(memory_space=pltpu.VMEM)
    n = max(Q - 1, 3)
    N = F // G if F % (G * LANES) == 0 else F
    results = pl.pallas_call(
        functools.partial(kernel, T, G),
        out_shape=(jax.ShapeDtypeStruct((S, F), f32),) * 4,
        in_specs=[pl.BlockSpec(memory_space=pltpu.SMEM), pl.BlockSpec(memory_space=pl.ANY)],
        out_specs=(vmem,) * 4,
        scratch_shapes=[
            V((R, F), bf16),
            V((NB, F + PAD, H), bf16),
            V((LAG, F), bf16),
            V((LAG, F), bf16),
            V((F + PAD, F), f32),
            V((2, Q, S, F), f32),
            V((PIECES, 2, Q, S, W), f32),
            V((Q, S, F), f32),
            V((PIECES, Q, S, W), f32),
            V((n, code_rows(S, F), LANES), i16),
            V((n, code_rows(S, F), LANES), i16),
            V((PIECES, Q, code_rows(S, W), LANES), i16),
            V((PIECES, Q, code_rows(S, W), LANES), i16),
            V((G, code_rows(S, N), LANES), i16),
            V((G, code_rows(S, N), LANES), i16),
            V((PIECES, G, code_rows(S, W), LANES), i16),
            V((2, code_rows(S, W), LANES), i16),
            V((4, code_rows(S, W), LANES), i16),
            V((G, code_rows(S, N), LANES), i16),
            V((2 * FR, LANES), f32),
            V((2 * FR, LANES), f32),
            V((Q, 2 * FR, LANES), f32),
            V((G, 2 * FR + 8, LANES), f32),
            V((2, Q, S, LANES), f32),
            V((2, S, F), f32),
            D((NB // LOAD,)),
            D((1,)),
            D((1,)),
            D((CUTS - 1,)),
            D((CUTS - 1,)),
            D((1,)),
            D((1 + PIECES,)),
            D((2 + PIECES,)),
            D((2 + PIECES,)),
            D((2 + PIECES,)),
            D((5 + PIECES,)),
            D((3,)),
            D((3,)),
        ],
        compiler_params=pltpu.CompilerParams(
            collective_id=0, has_side_effects=True, vmem_limit_bytes=48 * 1024 * 1024
        ),
    )(pair_count, frames)
    return pl.pallas_call(
        place,
        out_shape=(
            jax.ShapeDtypeStruct((1, S, F), f32),
            jax.ShapeDtypeStruct((1, S, F), f32),
            jax.ShapeDtypeStruct((S, F), f32),
            jax.ShapeDtypeStruct((S, F), f32),
        ),
        in_specs=[vmem] * 4,
        out_specs=(vmem,) * 4,
        compiler_params=pltpu.CompilerParams(vmem_limit_bytes=4 * 1024 * 1024),
    )(*results)


def solution(mesh):
    in_specs = (P("group", "tm", None), P("group"))
    out_specs = (P("group", "tm", None), P("group", "tm", None), P("tm", None), P("tm", None))
    body = functools.partial(on_device, mesh.shape["tm"], mesh.shape["group"])
    return jax.shard_map(
        body, mesh=mesh, in_specs=in_specs, out_specs=out_specs, check_vma=False
    )
```

```python
import functools

import jax
import jax.numpy as jnp
from jax import lax
from jax.experimental import pallas as pl
from jax.experimental.pallas import tpu as pltpu
from jax.sharding import PartitionSpec as P

LAG = 2048
MESH = pl.DeviceIdType.MESH
PAD = 16
CUTS = 4
PIECES = 2
LANES = 128
LEVELS = 32700.0
STEPS = 8.0
LEAST = 1e-30
LOAD = 8


def code_rows(S, W):
    return W // LANES * S + PAD


def encode(ref, block):
    S, W = block.shape
    top = jnp.maximum(jnp.max(jnp.abs(block), axis=0, keepdims=True), LEAST)
    power = jnp.ceil(STEPS * jnp.log2(top * (1.0 / LEVELS)))
    codes = jnp.round(block * (1.0 / jnp.exp2(power * (1.0 / STEPS)))).astype(jnp.int32)
    groups = W // LANES
    for g in range(groups):
        ref[g * S:(g + 1) * S, :] = codes[:, g * LANES:(g + 1) * LANES].astype(jnp.int16)
    row = lax.broadcasted_iota(jnp.int32, (PAD, LANES), 0)
    powers = jnp.zeros((PAD, LANES), jnp.float32)
    for g in range(groups):
        part = jnp.broadcast_to(power[:, g * LANES:(g + 1) * LANES], (PAD, LANES))
        powers = jnp.where(row == g, part, powers)
    ref[groups * S:, :] = powers.astype(jnp.int32).astype(jnp.int16)


def decode(ref, S):
    groups = (ref.shape[0] - PAD) // S
    powers = ref[groups * S:, :].astype(jnp.int32).astype(jnp.float32)
    units = jnp.exp2(powers * (1.0 / STEPS))
    parts = [
        ref[g * S:(g + 1) * S, :].astype(jnp.int32).astype(jnp.float32) * units[g:g + 1]
        for g in range(groups)
    ]
    return parts[0] if groups == 1 else jnp.concatenate(parts, axis=1)


def wide(column, width):
    return jnp.concatenate([column] * (width // LANES), axis=1)


def kernel(
    T, G, count_ref, frames_ref, gi_ref, gl_ref, pi_ref, po_ref,
    x, xt, head, tail, acc, ai, al, r1i, r1l, qi, ri, ql, rl, zi, zs, zl, zh, za, zg,
    s_own, s_mate, s_chip, s_grp, cols, fix,
    ld, nears, nearr, hs, hr, s1, e1, s2, e2, sz, ez, ss, es,
):
    F = frames_ref.shape[2]
    R = frames_ref.shape[1]
    H = LAG // CUTS
    NB = R // H
    W = F // PIECES
    S = F // T
    Q = T // 2
    FR = F // LANES
    NEAR = CUTS // 2
    f32 = jnp.float32
    me = lax.axis_index("tm")
    z = lax.axis_index("group")
    c = lax.rem(me, 2)
    q = lax.div(me, 2)
    partner = me + 1 - 2 * c
    count = count_ref[0]

    def remote(src, dst, a, b, dev):
        return pltpu.make_async_remote_copy(
            src_ref=src, dst_ref=dst, send_sem=a, recv_sem=b,
            device_id=dev, device_id_type=MESH,
        )

    def load(i):
        return pltpu.make_async_copy(
            frames_ref.at[0, pl.ds(i * LOAD * H, LOAD * H)], x.at[pl.ds(i * LOAD * H, LOAD * H)], ld.at[i]
        )

    def block(j):
        return x[pl.ds(pl.multiple_of(j * H, H), H), :]

    for i in range(NB // LOAD):
        load(i).start()

    barrier = pltpu.get_barrier_semaphore()
    for k in range(1, T):
        pl.semaphore_signal(
            barrier, inc=1, device_id={"tm": lax.rem(me + k, T)}, device_id_type=MESH
        )
    for k in range(1, G):
        pl.semaphore_signal(
            barrier, inc=1, device_id={"group": lax.rem(z + k, G)}, device_id_type=MESH
        )
    with jax.named_scope("t_barrier"):
        pl.semaphore_wait(barrier, T - 1 + G - 1)

    def kept(b):
        if T != 8:
            return CUTS // 2
        turn = lax.rem(b, 2) * (1 - lax.rem(lax.div(b, 2), 2))
        return CUTS // 2 + turn * (2 * lax.div(b, 4) - 1)

    before = lax.rem(me + T - 1, T)

    near_head = remote(
        frames_ref.at[0, pl.ds(0, NEAR * H)], head.at[pl.ds(0, NEAR * H)],
        nears.at[0], nearr.at[0], {"tm": partner},
    )
    near_tail = remote(
        frames_ref.at[0, pl.ds(R - LAG + NEAR * H, (CUTS - NEAR) * H)],
        tail.at[pl.ds(NEAR * H, (CUTS - NEAR) * H)],
        nears.at[0], nearr.at[0], {"tm": partner},
    )

    def send_head(j):
        return remote(
            frames_ref.at[0, pl.ds(j * H, H)], head.at[pl.ds(j * H, H)], hs.at[j], hr.at[j],
            {"tm": me - 1},
        )

    def send_tail(j):
        return remote(
            frames_ref.at[0, pl.ds(R - LAG + j * H, H)], tail.at[pl.ds(j * H, H)], hs.at[j - 1], hr.at[j - 1],
            {"tm": me + 1},
        )

    def far(act, now):
        for j in range(CUTS - 1):
            @pl.when((me > 0) & (c == 0) & (j < kept(before)) & now(kept(before) < NEAR))
            def _():
                act(send_head(j))

        for j in range(1, CUTS):
            @pl.when((me < T - 1) & (c == 1) & (j >= kept(me)) & now(kept(me) > NEAR))
            def _():
                act(send_tail(j))

    def sent(act):
        pl.when(c == 0)(lambda: act(near_tail))
        pl.when(c == 1)(lambda: act(near_head))

    far(lambda copy: copy.start(), jnp.logical_not)
    sent(lambda copy: copy.start())

    def put_transposed(block, base, slot):
        rows = lax.broadcasted_iota(jnp.int32, (H, LANES), 0) + base
        keep = jnp.where(rows < count, 1.0, 0.0).astype(jnp.bfloat16)
        xt[slot, 0:F, :] = (block * wide(keep, F)).T

    def put_masks(base, slot):
        frame = lax.broadcasted_iota(jnp.int32, (PAD, H), 1) + base
        kind = lax.broadcasted_iota(jnp.int32, (PAD, H), 0)
        first = jnp.where(kind == 0, 0, LAG)
        valid = (frame >= first) & (frame < first + count) & (kind < 2)
        xt[slot, F:, :] = jnp.where(valid, 1.0, 0.0).astype(jnp.bfloat16)

    def product(slot, block):
        return jnp.dot(xt[slot, 0:F, :], block, preferred_element_type=f32)

    acc[...] = jnp.zeros_like(acc)

    def inst_step(i, carry):
        @pl.when(lax.rem(2 * i, LOAD) == 0)
        def _():
            load(lax.div(2 * i, LOAD)).wait()

        for j in (2 * i, 2 * i + 1):
            put_transposed(block(j), me * R + j * H, j)
            put_masks(me * R + j * H, j)
        acc[...] += (
            jnp.dot(xt[2 * i], block(2 * i), preferred_element_type=f32)
            + jnp.dot(xt[2 * i + 1], block(2 * i + 1), preferred_element_type=f32)
        )
        return carry

    with jax.named_scope("t_inst"):
        lax.fori_loop(0, NB // 2, inst_step, 0)
    for d in range(T):
        ai[d % 2, d // 2] = acc[d * S:(d + 1) * S, :]
    for k in range(2):
        for j in range(FR):
            s_own[k * FR + j:k * FR + j + 1, :] = acc[F + k:F + k + 1, j * LANES:(j + 1) * LANES]
    p1i = remote(ai.at[1 - c], r1i, s1.at[0], e1.at[0], {"tm": partner})
    p1i.start()
    mate = remote(s_own, s_mate, ss.at[0], es.at[0], {"tm": partner})
    mate.start()

    acc[...] = jnp.zeros_like(acc)

    def lag_step(i, carry):
        j = 2 * i
        acc[0:F, :] += product(j, block(j + CUTS)) + product(j + 1, block(j + 1 + CUTS))
        return carry

    with jax.named_scope("t_lag"):
        lax.fori_loop(0, (NB - CUTS) // 2, lag_step, 0)
    far(lambda copy: copy.start(), lambda late: late)

    def clip(v, top):
        return jnp.minimum(jnp.maximum(v, 0), top)

    def vector(n):
        return jnp.broadcast_to(n, (1, LANES)).astype(f32)

    def weights(chip):
        a = chip * 2 * R
        nx = clip(count - a, 2 * R)
        ny = clip(count + LAG - a, 2 * R) - clip(LAG - a, 2 * R)
        low = jnp.where(chip > 0, kept(2 * chip - 1) * H - LAG, 0)
        high = jnp.where(chip < Q - 1, kept(2 * chip + 1) * H - LAG, 0)
        pairs = clip(count - a - low, 2 * R + high - low)
        vx, vy = vector(jnp.maximum(nx, 1)), vector(jnp.maximum(ny, 1))
        return 1.0 / vx, vector(pairs) / (vx * vy)

    lanes = lax.broadcasted_iota(jnp.int32, (S, LANES), 1)
    rows = lax.broadcasted_iota(jnp.int32, (S, LANES), 0)

    def upright(row, offset):
        picked = jnp.where(lanes == rows + offset, jnp.broadcast_to(row, (S, LANES)), 0.0)
        return jnp.broadcast_to(jnp.sum(picked, axis=1, keepdims=True), (S, LANES))

    def along(ref, kind):
        return jnp.concatenate([ref[kind * FR + j:kind * FR + j + 1, :] for j in range(FR)], axis=1)

    class Group:
        def __init__(self, a, b, like, n):
            self.pairs, self.a, self.b, self.like, self.n = [], a, b, like, n

        def send(self, src, dst, dev):
            remote(src, dst, self.a, self.b, dev).start()

        def whole(self):
            ref = self.like.at[pl.ds(0, self.n)]
            return remote(ref, ref, self.a, self.b, {"tm": partner})

        def wait_recv(self):
            self.whole().wait_recv()

        def wait_send(self):
            self.whole().wait_send()

    with jax.named_scope("t_p1i"):
        mate.wait_recv()
        s_chip[q] = s_own[...] + s_mate[...]
        chips = Group(ss.at[1], es.at[1], s_chip, Q - 1)
        for k in range(1, Q):
            chips.send(s_chip.at[q], s_chip.at[q], {"tm": 2 * lax.rem(q + k, Q) + c})
        wx, wl = weights(q)
        mine = s_chip.at[q]
        for k in range(Q):
            at = 2 * k * S
            col = upright(mine[at // LANES:at // LANES + 1, :], at % LANES + c * S)
            cols[0, k] = col * wx
            cols[1, k] = col * wl
        p1i.wait_recv()
        sx = along(mine, 0)
        for k in range(Q):
            ai[c, k] = ai[c, k] + r1i[k] - wide(cols[0, k], F) * sx

    square = Q == 4
    with jax.named_scope("t_inst_send"):
        if square:
            side, level = lax.rem(q, 2), lax.div(q, 2)
            across = q + 1 - 2 * side
            for k in range(2):
                encode(qi.at[k], ai[c, 2 - 2 * level + k])
            over = remote(
                qi.at[pl.ds(0, 2)], ri.at[pl.ds(0, 2)], s2.at[0], e2.at[0],
                {"tm": 2 * lax.rem(q + 2, Q) + c},
            )
            over.start()
            p2i = remote(qi.at[2], ri.at[2], s2.at[1], e2.at[1], {"tm": 2 * across + c})
        else:
            p2i = Group(s2.at[1], e2.at[1], ri, Q - 1)
            for k in range(1, Q):
                q2 = lax.rem(q + k, Q)
                encode(qi.at[k - 1], ai[c, q2])
                p2i.send(qi.at[k - 1], ri.at[k - 1], {"tm": 2 * q2 + c})

    def take_head(j):
        acc[0:F, :] += product(NB - CUTS + j, head[pl.ds(pl.multiple_of(j * H, H), H), :])

    def take_tail(j):
        put_transposed(tail[pl.ds(pl.multiple_of(j * H, H), H), :], me * R - LAG + j * H, j)
        acc[0:F, :] += product(j, block(j))

    def near_heads():
        near_head.wait_recv()

        def step(j, carry):
            take_head(j)
            return carry

        lax.fori_loop(0, NEAR, step, 0)

    def near_tails():
        near_tail.wait_recv()

        def step(j, carry):
            take_tail(j)
            return carry

        lax.fori_loop(NEAR, CUTS, step, 0)

    def relay_instant():
        over.wait_recv()
        for k in range(2):
            ai[c, 2 * level + k] += decode(ri.at[k], S)
        encode(qi.at[2], ai[c, across])
        p2i.start()

    def far_heads():
        def step(j, carry):
            send_head(j).wait_recv()
            take_head(j)
            return carry

        lax.fori_loop(0, kept(me) - 1, step, 0)
        if square:
            pl.when(kept(me) > 1)(relay_instant)
        step(kept(me) - 1, 0)

    def far_tails():
        def step(j, carry):
            send_tail(j).wait_recv()
            take_tail(j)
            return carry

        lax.fori_loop(kept(before), CUTS - 1, step, 0)
        if square:
            pl.when(kept(before) < CUTS - 1)(relay_instant)
        step(CUTS - 1, 0)

    with jax.named_scope("t_halo_near"):
        pl.when(c == 0)(near_heads)
        pl.when(c == 1)(near_tails)
    with jax.named_scope("t_halo_far"):
        has_heads = (me < T - 1) & (c == 1)
        has_tails = (me > 0) & (c == 0)
        pl.when(has_heads)(far_heads)
        pl.when(has_tails)(far_tails)

    with jax.named_scope("t_lag_out"):
        p1l = []
        for h in range(PIECES):
            for d in range(T):
                al[h, d % 2, d // 2] = acc[d * S:(d + 1) * S, h * W:(h + 1) * W]
            p1l.append(
                remote(al.at[h, 1 - c], r1l.at[h], s1.at[0], e1.at[1 + h], {"tm": partner})
            )
            p1l[h].start()

    with jax.named_scope("t_inst_x"):
        if square:
            early = (has_heads & (kept(me) > 1)) | (has_tails & (kept(before) < CUTS - 1))
            pl.when(jnp.logical_not(early))(relay_instant)

    with jax.named_scope("t_p1l"):
        p2l = [Group(s2.at[2 + h], e2.at[2 + h], rl.at[h], Q - 1) for h in range(PIECES)]

        def spread(h, chip):
            @pl.when(chip != q)
            def _():
                sy = along(mine, 1)[:, h * W:(h + 1) * W]
                encode(
                    ql.at[h, chip], al[h, c, chip] + r1l[h, chip] - wide(cols[1, chip], W) * sy
                )
                p2l[h].send(ql.at[h, chip], rl.at[h, q], {"tm": 2 * chip + c})

        for h in range(PIECES):
            p1l[h].wait_recv()
            for i in range(Q):
                spread(h, i if h == 0 else jnp.where(c == 0, i, Q - 1 - i))
            sy = along(mine, 1)[:, h * W:(h + 1) * W]
            al[h, c, q] = al[h, c, q] + r1l[h, q] - wide(cols[1, q], W) * sy

    with jax.named_scope("t_sums"):
        chips.wait_recv()

        at = lax.div(me * S, LANES)
        off = lax.rem(me * S, LANES)

        def outer(ref, kind, scale):
            return wide(upright(ref[pl.ds(at, 1), :], off) * scale, F) * along(ref, kind)

        total = s_chip[0]
        for k in range(1, Q):
            total = total + s_chip[k]
        s_grp[z, 0:2 * FR, :] = total
        s_grp[z, 2 * FR:, :] = jnp.broadcast_to(vector(count), (8, LANES))
        groups = Group(ss.at[2], es.at[2], s_grp, G - 1)
        for k in range(1, G):
            groups.send(s_grp.at[z], s_grp.at[z], {"group": lax.rem(z + k, G)})
        number = vector(count)
        for kind in range(2):
            term = -outer(s_grp.at[z], kind, 1.0 / number)
            for k in range(Q):
                term = term + outer(s_chip.at[k], kind, weights(k)[kind])
            fix[kind] = term
        count_f = wide(number, F)

    def to_groups(group, buf):
        for i in range(G):
            w = jnp.where(c == 0, i, G - 1 - i)

            @pl.when(w != z)
            def _():
                group.send(buf.at[z], buf.at[z], {"group": w})

    shares = G if F % (G * LANES) == 0 else 1
    N = F // shares
    with jax.named_scope("t_zi"):
        p2i.wait_recv()
        total = ai[c, q] + fix[0]
        for k in ((2,) if square else range(Q - 1)):
            total = total + decode(ri.at[k], S)
        gi_ref[...] = total / count_f
        part_sums = Group(sz.at[0], ez.at[0], zs, G - 1)
        full_sums = Group(sz.at[1], ez.at[1], zi, G - 1)
        if shares == G:
            for w in range(G):
                cut = total[:, w * N:(w + 1) * N]

                @pl.when(w != z)
                def _():
                    encode(zi.at[w], cut)
                    part_sums.send(zi.at[w], zs.at[z], {"group": w})

                @pl.when(w == z)
                def _():
                    ai[c, q, :, 0:N] = cut
        else:
            encode(zi.at[z], total)
            to_groups(full_sums, zi)

    hub = G == 4
    zl_groups = []
    if hub:
        inner = (z == 1) | (z == 2)
        neighbour = jnp.where(z < 2, 1, 2)
        direct = Group(sz.at[2], ez.at[6], za, G - 1)

        def inward(slot):
            return remote(za.at[slot], za.at[slot], sz.at[2], ez.at[2], {"group": neighbour})

        def onward(k, w):
            return remote(zh.at[k], zh.at[k], sz.at[2], ez.at[4 + k], {"group": w})

    def lag_session(h):
        with jax.named_scope("t_p2l"):
            p2l[h].wait_recv()
            part = slice(h * W, (h + 1) * W)
            total = al[h, c, q] + fix[1, :, part]
            for k in range(1, Q):
                total = total + decode(rl.at[h, lax.rem(q + k, Q)], S)
            gl_ref[:, part] = total / count_f[:, part]
            if hub and h == 0:
                encode(za.at[z], total)

                @pl.when(jnp.logical_not(inner))
                def _():
                    inward(z).start()

                @pl.when(z > 0)
                def _():
                    direct.send(za.at[z], za.at[z], {"group": 0})

            else:
                encode(zl.at[h, z], total)
                zl_groups.append(Group(sz.at[2 + h], ez.at[2 + h], zl.at[h], G - 1))
                to_groups(zl_groups[-1], zl.at[h])

    lag_session(0)
    if shares == G:
        with jax.named_scope("t_zi_share"):
            part_sums.wait_recv()
            total = ai[c, q, :, 0:N]
            for k in range(1, G):
                total = total + decode(zs.at[lax.rem(z + k, G)], S)
            encode(zg.at[z], total)
            full_sums = Group(sz.at[1], ez.at[1], zg, G - 1)
            to_groups(full_sums, zg)
    for h in range(1, PIECES):
        lag_session(h)
    if hub:
        with jax.named_scope("t_hub"):
            @pl.when(inner)
            def _():
                inward(3 * (z - 1)).wait_recv()

            pl.when(z == 0)(direct.wait_recv)
            for k in range(2):
                @pl.when((z == 0) | (z == 1 + k))
                def _():
                    encode(zh.at[k], decode(za.at[2 * k], S) + decode(za.at[2 * k + 1], S))

                @pl.when(z == 1 + k)
                def _():
                    for w in (2 - k, 3):
                        onward(k, w).start()

    with jax.named_scope("t_pool"):
        groups.wait_recv()
        everyone = s_grp[0]
        for k in range(1, G):
            everyone = everyone + s_grp[k]
        s_mate[...] = everyone[0:2 * FR]
        all_n = everyone[2 * FR:2 * FR + 1]
        for kind in range(2):
            term = -outer(s_mate, kind, 1.0 / all_n)
            for k in range(G):
                term = term + outer(s_grp.at[k], kind, 1.0 / s_grp[k, 2 * FR:2 * FR + 1, :])
            fix[kind] = term
        whole_f = wide(all_n, F)

    def pooled(h):
        part = slice(h * W, (h + 1) * W)
        total = fix[1, :, part]
        if hub and h == 0:
            for k in range(2):
                total = total + decode(zh.at[k], S)
        else:
            for k in range(G):
                total = total + decode(zl.at[h, k], S)
        po_ref[:, part] = total / whole_f[:, part]

    for h in range(1 if hub else 0, PIECES):
        with jax.named_scope("t_zl_in"):
            zl_groups[h - PIECES].wait_recv()
            pooled(h)
    if hub:
        with jax.named_scope("t_hub_in"):
            for k in range(2):
                pl.when((z == 3) | (z == 2 - k))(onward(k, 3).wait_recv)
            pooled(0)

    with jax.named_scope("t_zi_in"):
        full_sums.wait_recv()
        if shares == G:
            for w in range(G):
                part = slice(w * N, (w + 1) * N)
                pi_ref[:, part] = (fix[0, :, part] + decode(zg.at[w], S)) / whole_f[:, part]
        else:
            total = fix[0]
            for k in range(G):
                total = total + decode(zi.at[k], S)
            pi_ref[...] = total / whole_f

    with jax.named_scope("t_end"):
        sent(lambda copy: copy.wait_send())
        far(lambda copy: copy.wait_send(), lambda late: late)
        far(lambda copy: copy.wait_send(), jnp.logical_not)
        if square:
            over.wait_send()
        if shares == G:
            part_sums.wait_send()
        if hub:
            for n, which in ((1, z == 0), (2, z == 3), (3, inner)):
                pl.when(which)(Group(sz.at[2], ez.at[6], za, n).wait_send)
        remote(ai, ai, s1.at[0], e1.at[0], {"tm": partner}).wait_send()
        for copy in [mate, chips, groups, p2i, *p2l, full_sums, *zl_groups]:
            copy.wait_send()


def place(gi, gl, pi, po, gi_out, gl_out, pi_out, po_out):
    gi_out[0] = gi[...]
    gl_out[0] = gl[...]
    pi_out[...] = pi[...]
    po_out[...] = po[...]


def on_device(T, G, frames, pair_count):
    _, R, F = frames.shape
    S, Q, H, W = F // T, T // 2, LAG // CUTS, F // PIECES
    NB = R // H
    FR = F // LANES
    f32, bf16, i16 = jnp.float32, jnp.bfloat16, jnp.int16
    V, D = pltpu.VMEM, pltpu.SemaphoreType.DMA
    vmem = pl.BlockSpec(memory_space=pltpu.VMEM)
    n = max(Q - 1, 3)
    N = F // G if F % (G * LANES) == 0 else F
    results = pl.pallas_call(
        functools.partial(kernel, T, G),
        out_shape=(jax.ShapeDtypeStruct((S, F), f32),) * 4,
        in_specs=[pl.BlockSpec(memory_space=pltpu.SMEM), pl.BlockSpec(memory_space=pl.ANY)],
        out_specs=(vmem,) * 4,
        scratch_shapes=[
            V((R, F), bf16),
            V((NB, F + PAD, H), bf16),
            V((LAG, F), bf16),
            V((LAG, F), bf16),
            V((F + PAD, F), f32),
            V((2, Q, S, F), f32),
            V((PIECES, 2, Q, S, W), f32),
            V((Q, S, F), f32),
            V((PIECES, Q, S, W), f32),
            V((n, code_rows(S, F), LANES), i16),
            V((n, code_rows(S, F), LANES), i16),
            V((PIECES, Q, code_rows(S, W), LANES), i16),
            V((PIECES, Q, code_rows(S, W), LANES), i16),
            V((G, code_rows(S, N), LANES), i16),
            V((G, code_rows(S, N), LANES), i16),
            V((PIECES, G, code_rows(S, W), LANES), i16),
            V((2, code_rows(S, W), LANES), i16),
            V((4, code_rows(S, W), LANES), i16),
            V((G, code_rows(S, N), LANES), i16),
            V((2 * FR, LANES), f32),
            V((2 * FR, LANES), f32),
            V((Q, 2 * FR, LANES), f32),
            V((G, 2 * FR + 8, LANES), f32),
            V((2, Q, S, LANES), f32),
            V((2, S, F), f32),
            D((NB // LOAD,)),
            D((1,)),
            D((1,)),
            D((CUTS - 1,)),
            D((CUTS - 1,)),
            D((1,)),
            D((1 + PIECES,)),
            D((2 + PIECES,)),
            D((2 + PIECES,)),
            D((2 + PIECES,)),
            D((5 + PIECES,)),
            D((3,)),
            D((3,)),
        ],
        compiler_params=pltpu.CompilerParams(
            collective_id=0, has_side_effects=True, vmem_limit_bytes=48 * 1024 * 1024
        ),
    )(pair_count, frames)
    return pl.pallas_call(
        place,
        out_shape=(
            jax.ShapeDtypeStruct((1, S, F), f32),
            jax.ShapeDtypeStruct((1, S, F), f32),
            jax.ShapeDtypeStruct((S, F), f32),
            jax.ShapeDtypeStruct((S, F), f32),
        ),
        in_specs=[vmem] * 4,
        out_specs=(vmem,) * 4,
        compiler_params=pltpu.CompilerParams(vmem_limit_bytes=4 * 1024 * 1024),
    )(*results)


def solution(mesh):
    in_specs = (P("group", "tm", None), P("group"))
    out_specs = (P("group", "tm", None), P("group", "tm", None), P("tm", None), P("tm", None))
    body = functools.partial(on_device, mesh.shape["tm"], mesh.shape["group"])
    return jax.shard_map(
        body, mesh=mesh, in_specs=in_specs, out_specs=out_specs, check_vma=False
    )
```
